32 devices in a mesh: row: 2 (over y), col: 16 (over z, x, core).
Axes of the slice: x: 2, y: 2, z: 4, core: 2. Of those that a mesh axis runs over, the one named last changes fastest.
Arguments:
- a_blocks: bfloat16 [2, 16, 320, 64, 64], P('row', 'col'), may hold values from -1.25 to 1.25
- block_rows: int32 [2, 16, 320], P('row', 'col'), may hold values from 0 to 255
- block_cols: int32 [2, 16, 320], P('row', 'col'), may hold values from 0 to 31
- block_count: int32 [2, 16], P('row', 'col'), may hold values from 160 to 320, as said below
- restrict: bfloat16 [512, 64, 64], P(('row', 'col')), may hold values from -0.75 to 0.75
- interp: bfloat16 [512, 64, 64], P('col', 'row'), may hold values from -0.75 to 0.75
- aggregate: int32 [512], replicated, may hold values from 0 to 15, as said below
- owner: int32 [16], replicated, may hold values from 0 to 15, each once
Outputs:
- coarse: float32 [16, 16, 64, 64], P('col')
The draws below stay inside these ranges and needn't reach their ends.
Inputs may be any that keep to these rules, and one draw needn't show every extreme that they name: `block_count`: at least one device holds 320 live blocks in every draw. aggregate[i] differs from i * 16 // 512 by at most one, and by exactly one for some block in every draw.
All inputs are finite; a program needn't handle non-finite values.
Results may differ from the reference program's by a relative error of at most 0.0029.
Values may be sent and summed in bfloat16 or wider, within the bound.
A program may use at most 128 MiB of HBM per device.

```python
import jax
import jax.numpy as jnp
from jax import lax

BS = 64
RB = 256
NNZ_DEV = 320
NFB = 512
CB = 32
NA = 16
N_ROW = 2
N_COL = 16


def draw_block_count(key, part):
    first, second = jax.random.split(key)
    counts = jax.random.randint(first, (N_ROW * N_COL,), NNZ_DEV // 2, NNZ_DEV + 1)
    fullest = jax.random.randint(second, (), 0, N_ROW * N_COL)
    counts = jnp.where(jnp.arange(N_ROW * N_COL) == fullest, NNZ_DEV, counts)
    return counts.reshape(N_ROW, N_COL).astype(jnp.int32)


def draw_aggregate(key, part):
    coins = jax.random.randint(jax.random.fold_in(key, 17), (NFB,), 0, 2)
    index = jnp.arange(NFB, dtype=jnp.int32)
    per_agg = NFB // NA
    base = index // per_agg
    place = index % per_agg
    shift = jnp.where((place == 0) & (coins == 1), -1, 0)
    shift = jnp.where((place == per_agg - 1) & (coins == 1), 1, shift)
    shift = jnp.where(index == per_agg, -1, shift)
    return jnp.clip(base + shift, 0, NA - 1).astype(jnp.int32)


def plant(values, own_key, smallest, top_value):
    extent = values.shape
    spot = [jax.random.randint(jax.random.fold_in(own_key, axis), (), 0, extent[axis]) for axis in range(len(extent))]
    values = values.at[tuple(spot)].set(smallest)
    longest = extent.index(max(extent))
    spot[longest] = (spot[longest] + 1) % extent[longest]
    return values.at[tuple(spot)].set(top_value)


def shard_levels(own_key, dims, cuts, least, top_value):
    def one(dim, parts):
        steps = jax.random.uniform(jax.random.fold_in(jax.random.fold_in(own_key, 6), dim), (parts,), jnp.float32, least / len(cuts), top_value / len(cuts))
        return jnp.repeat(jnp.exp(steps), dims[dim] // parts).reshape((-1,) + (1,) * (len(dims) - dim - 1))

    level = one(*cuts[0])
    for cut in cuts[1:]:
        level = level * one(*cut)
    return level


def gaussian(own_key, dims, scale, reach, pieces=(), held_as=jnp.bfloat16):
    level = shard_levels(own_key, dims, pieces, -0.22, 0.18) if pieces else 1.0
    drawn = jax.random.normal(own_key, dims, jnp.float32) * scale * level
    return jnp.minimum(jnp.maximum(drawn, -reach), reach).astype(held_as)


def setup_inputs(seed: int = 0) -> dict:
    keys = jax.random.split(jax.random.key(seed), 9)
    return {
        "a_blocks": gaussian(keys[0], (N_ROW, N_COL, NNZ_DEV, BS, BS), (0.64 / BS ** 0.5), 1.25, ((0, 2), (1, 16))),
        "block_rows": plant(jax.random.randint(keys[1], (N_ROW, N_COL, NNZ_DEV), 0, RB), jax.random.fold_in(keys[1], 1), 0, RB - 1).astype(jnp.int32),
        "block_cols": plant(jax.random.randint(keys[2], (N_ROW, N_COL, NNZ_DEV), 0, CB), jax.random.fold_in(keys[2], 1), 0, CB - 1).astype(jnp.int32),
        "block_count": draw_block_count(jax.random.fold_in(keys[8], 71), 0),
        "restrict": gaussian(keys[4], (NFB, BS, BS), BS ** -0.5, 0.75, ((0, 32),)),
        "interp": gaussian(keys[5], (NFB, BS, BS), BS ** -0.5, 0.75, ((0, 16), (1, 2))),
        "aggregate": draw_aggregate(jax.random.fold_in(keys[8], 71), 0),
        "owner": jax.random.permutation(keys[7], NA).astype(jnp.int32),
    }


def reference(a_blocks, block_rows, block_cols, block_count, restrict, interp, aggregate, owner):
    flat_blocks = a_blocks.reshape(N_ROW * N_COL, NNZ_DEV, BS, BS)
    flat_rows = block_rows.reshape(N_ROW * N_COL, NNZ_DEV)
    flat_cols = block_cols.reshape(N_ROW * N_COL, NNZ_DEV)
    flat_count = block_count.reshape(N_ROW * N_COL)
    device_ids = jnp.arange(N_ROW * N_COL, dtype=jnp.int32)

    def one_device(total, items):
        blocks, rows, cols, count, device = items
        row_index = device // N_COL
        col_index = device % N_COL
        fine_rows = row_index * RB + rows
        fine_cols = col_index * CB + cols
        product = jnp.einsum("pxy,pyz->pxz", blocks.astype(jnp.float32), interp[fine_cols].astype(jnp.float32)).astype(jnp.bfloat16)
        term = jnp.einsum("pxy,pyz->pxz", restrict[fine_rows].astype(jnp.float32), product.astype(jnp.float32))
        live = (jnp.arange(NNZ_DEV, dtype=jnp.int32) < count).astype(jnp.float32)
        term = term * live[:, None, None]
        pair_ids = owner[aggregate[fine_rows]] * NA + aggregate[fine_cols]
        summed = jax.ops.segment_sum(term.reshape(NNZ_DEV, BS * BS), pair_ids, NA * NA)
        return total + summed, None

    start = jnp.zeros((NA * NA, BS * BS), jnp.float32)
    total, _ = lax.scan(one_device, start, (flat_blocks, flat_rows, flat_cols, flat_count, device_ids))
    return total.reshape(NA, NA, BS, BS)
```

```python
import functools

import jax
import jax.numpy as jnp
from jax import lax
from jax.experimental import pallas as pl
from jax.experimental.pallas import tpu as pltpu
from jax.sharding import PartitionSpec as P

MESH = pl.DeviceIdType.MESH
CORES = 2
DEPTH = 4
CHUNKS = 4
GROUP = 32
SLOT_BITS = 9
COL_BITS = 6
KEY_SHIFT = SLOT_BITS + COL_BITS


def coarse_kernel(
    n_row, n_col, rows_hbm, cols_hbm, count_hbm, agg_hbm, owner_hbm, r_hbm, p_hbm, a_hbm, out_ref,
    rows_ref, cols_ref, count_ref, agg_ref, owner_ref, r_ref, p_ref, a_ref,
    rg_ref, pg_ref, flat, wide, sums, turned, v_col, rank_col, v_tab, last_tab, v_smem, last_smem, part,
    edge_out, edge_sib, edge_in, mid, mid_in, full, outgoing, incoming, inverse,
    load_sem, tab_sem, right_sem, left_sem, sib_sem, recv_sem, psend_sem, precv_sem,
    ssend_sem, srecv_sem, esend_sem, erecv_sem, msend_sem, mrecv_sem, send_sem, recv2_sem,
):
    width = n_col // (CORES * DEPTH)
    chips = n_col // CORES
    half_ring = chips // 2
    me = lax.axis_index("col")
    row = lax.axis_index("row")
    z = me // (width * CORES)
    x = lax.rem(me // CORES, width)
    k = lax.rem(me, CORES)
    sibling = me + 1 - 2 * k
    beside = me - 1 + 2 * k
    has_beside = (beside >= 0) & (beside < n_col)
    other_row = [lax.rem(row + d, n_row) for d in range(1, n_row)]

    back = DEPTH - 1 - z
    spot = jnp.where(
        x == 0, z, DEPTH + back * (width - 1) + jnp.where(lax.rem(back, 2) == 0, x - 1, width - 1 - x)
    )

    def chip_at(offset):
        s = lax.rem(spot + offset + chips, chips)
        b = (s - DEPTH) // (width - 1)
        i = lax.rem(s - DEPTH, width - 1)
        far = (DEPTH - 1 - b) * width + jnp.where(lax.rem(b, 2) == 0, i + 1, width - 1 - i)
        return jnp.where(s < DEPTH, s * width, far)

    def shard_at(offset):
        return chip_at(offset) * CORES + k

    right = shard_at(1)
    left = shard_at(-1)

    nb = r_ref.shape[0]
    tiles = nb // 2
    half_p = p_ref.shape[0] // 2
    piece = p_ref.shape[1]
    nj = p_ref.shape[0]
    slots = a_ref.shape[2]
    panel = nb * n_col
    per_agg = agg_ref.shape[0] // n_col
    row_width = part.shape[0] // 64

    loads = [
        pltpu.make_async_copy(src, dst, load_sem.at[i])
        for i, (src, dst) in enumerate(
            [
                (r_hbm, r_ref), (p_hbm, p_ref), (rows_hbm, rows_ref), (cols_hbm, cols_ref), (count_hbm, count_ref),
                (agg_hbm, agg_ref), (owner_hbm, owner_ref), (a_hbm, a_ref),
            ]
        )
    ]
    for load in loads:
        load.start()
    load_r, load_p, load_rows, load_cols, load_count, load_agg, load_owner, load_a = loads

    barrier = pltpu.get_barrier_semaphore()

    def greet(dev):
        pl.semaphore_signal(barrier, inc=1, device_id=dev, device_id_type=MESH)

    def greet_row(i, _):
        greet((row, lax.rem(me + i, n_col)))
        return 0

    lax.fori_loop(1, n_col, greet_row, 0)
    for o in other_row:
        greet((o, me))

    @pl.when(has_beside)
    def _():
        for o in other_row:
            greet((o, beside))

    load_r.wait()
    for j in range(tiles):
        rg_ref[me, j] = jnp.concatenate([r_ref[2 * j], r_ref[2 * j + 1]], axis=1)
    load_p.wait()
    for j in range(half_p):
        pg_ref[row, j, :, 0:64] = p_ref[j]
        pg_ref[row, j, :, 64:128] = p_ref[j + half_p]

    pl.semaphore_wait(barrier, n_col - 1 + len(other_row) + jnp.where(has_beside, len(other_row), 0))

    size = tiles // CHUNKS
    half = CHUNKS // 2

    def ring(shard, c, sem, target):
        piece_of = rg_ref.at[shard, pl.ds(c * size, size)]
        return pltpu.make_async_remote_copy(
            src_ref=piece_of, dst_ref=piece_of, send_sem=sem.at[shard, c], recv_sem=recv_sem.at[shard, c],
            device_id=(row, target), device_id_type=MESH,
        )

    def go_right(shard, c):
        return ring(shard, c, right_sem, right)

    def go_left(shard, c):
        return ring(shard, c, left_sem, left)

    def go_over(shard):
        return pltpu.make_async_remote_copy(
            src_ref=rg_ref.at[shard], dst_ref=rg_ref.at[shard], send_sem=sib_sem.at[shard], recv_sem=recv_sem.at[shard, 0],
            device_id=(row, sibling), device_id_type=MESH,
        )

    def pcopy(way, target):
        return pltpu.make_async_remote_copy(
            src_ref=pg_ref.at[row], dst_ref=pg_ref.at[row], send_sem=psend_sem.at[way], recv_sem=precv_sem.at[row],
            device_id=(target, me), device_id_type=MESH,
        )

    for c in range(CHUNKS):
        go_right(me, c).start()
        go_left(me, (c + half) % CHUNKS).start()
    for w, o in enumerate(other_row):
        pcopy(w, o).start()
    go_over(me).start()

    def pass_on(d, c):
        back_c = (c + half) % CHUNKS
        onward = d < half_ring - 1 or c < half
        s = shard_at(-d)
        go_right(s, c).wait_recv()
        if onward:
            go_right(s, c).start()
        s = shard_at(d)
        go_left(s, back_c).wait_recv()
        if onward:
            go_left(s, back_c).start()
        if c == CHUNKS - 1:
            go_over(shard_at(-d)).start()
            go_over(shard_at(d)).start()

    def far_end():
        s = shard_at(half_ring)
        for c in range(CHUNKS):
            go_right(s, c).wait_recv()
        go_over(s).start()

    tile_ends = [(s, min(s + 128, slots)) for s in range(0, slots, 128)]

    def turn(lo, hi):
        def body(i, _):
            for s, e in tile_ends:
                tall = jnp.concatenate([a_ref[i, :, s:e], a_ref[i + 32, :, s:e]], axis=0)
                flat[s:e, i, :] = tall.T.astype(jnp.float32)
            return 0

        lax.fori_loop(lo, hi, body, 0)

    def tables():
        load_rows.wait()
        load_cols.wait()
        load_count.wait()
        load_agg.wait()
        cols = cols_ref[...]
        off = jnp.zeros_like(cols)
        for j in range(nj):
            off = jnp.where(cols == j, agg_ref[me * nj + j] - (me - 1), off)
        slot = lax.broadcasted_iota(jnp.int32, (1, slots), 1)
        key = jnp.where(slot < count_ref[0, 0], rows_ref[...] * 4 + off, panel * 4)
        v = (key * 2**COL_BITS + cols) * 2**SLOT_BITS + slot
        for s, e in tile_ends:
            v_col[s:e, :] = jnp.broadcast_to(v[:, s:e], (128, e - s)).T
        for s, e in tile_ends:
            below = (v_col[:, 0 : e - s] < v[:, s:e]).astype(jnp.int32)
            rank = jnp.sum(below, axis=0, keepdims=True)
            rank_col[s:e, :] = jnp.broadcast_to(rank, (128, e - s)).T
        for s, e in tile_ends:
            place = lax.broadcasted_iota(jnp.int32, (1, e - s), 1) + s
            hit = rank_col[:, 0 : e - s] == place
            v_tab[:, s:e] = jnp.sum(jnp.where(hit, v_col[:, 0 : e - s], 0), axis=0, keepdims=True)
        for s in range(0, panel * 4, 128):
            place = lax.broadcasted_iota(jnp.int32, (1, 128), 1) + s
            keys = v_col[...] >> KEY_SHIFT
            upto = jnp.sum((keys <= place).astype(jnp.int32), axis=0, keepdims=True)
            under = jnp.sum((keys < place).astype(jnp.int32), axis=0, keepdims=True)
            last_tab[:, s : s + 128] = jnp.where(upto > under, upto, 0)
        copies = [
            pltpu.make_async_copy(v_tab, v_smem, tab_sem.at[0]), pltpu.make_async_copy(last_tab, last_smem, tab_sem.at[1])
        ]
        for c in copies:
            c.start()
        for c in copies:
            c.wait()

    def widen():
        for o in other_row:
            pltpu.make_async_remote_copy(
                src_ref=pg_ref.at[o], dst_ref=pg_ref.at[o], send_sem=psend_sem.at[0], recv_sem=precv_sem.at[o],
                device_id=(o, me), device_id_type=MESH,
            ).wait_recv()
        wide[...] = jnp.zeros_like(wide)

        def body(j, _):
            for r in range(n_row):
                lo, hi = r * piece, (r + 1) * piece
                both = pg_ref[r, j]
                wide[j, lo:hi, 0:64] = both[:, 0:64]
                wide[j, 64 + lo : 64 + hi, 64:128] = both[:, 0:64]
                wide[j + half_p, lo:hi, 0:64] = both[:, 64:128]
                wide[j + half_p, 64 + lo : 64 + hi, 64:128] = both[:, 64:128]
            return 0

        lax.fori_loop(0, half_p, body, 0, unroll=2)
        sums[0] = jnp.zeros((32, 128), jnp.bfloat16)
        turned[0] = jnp.zeros((32, 128), jnp.bfloat16)

    def multiply(lo, hi, run):
        def body(g, run):
            base = g * GROUP
            made = []
            for u in range(GROUP):
                v = v_smem[0, base + u]
                left_side = flat[v & (2**SLOT_BITS - 1)].astype(jnp.bfloat16)
                right_side = wide[(v >> SLOT_BITS) & (2**COL_BITS - 1)]
                product = jnp.dot(left_side, right_side, preferred_element_type=jnp.float32).astype(jnp.bfloat16)
                made.append(product)
            before = v_smem[0, jnp.maximum(base - 1, 0)] >> KEY_SHIFT
            for u in range(GROUP):
                now = v_smem[0, base + u] >> KEY_SHIFT
                run = run * jnp.where(now == before, 1.0, 0.0) + made[u].astype(jnp.float32)
                before = now
                both = run.astype(jnp.bfloat16)
                sums[base + u + 1] = both
                turned[base + u + 1] = jnp.concatenate([both[:, 64:128], both[:, 0:64]], axis=1)
            return run

        return lax.fori_loop(lo, hi, body, run)

    left_half = lax.broadcasted_iota(jnp.int32, (32, 128), 1) < 64
    left_row = lax.broadcasted_iota(jnp.int32, (16, 128), 1) < 64

    def shard_of(i):
        far = jnp.maximum(i - 2, 0)
        step = jnp.where(i < 2, 0, far // 4 + 1)
        offset = jnp.where(lax.rem(far, 4) < 2, -step, step)
        return chip_at(offset) * CORES + jnp.where(lax.rem(i, 2) == 0, k, 1 - k)

    def dense(lo, hi):
        def body(i, _):
            s = shard_of(i)
            base = s * nb // per_agg
            floor = row * (n_col // n_row) + base - 1
            total = None
            for t in range(tiles // 2):
                lefts = [[], [], []]
                rights = []
                for h in range(2):
                    j = 2 * t + h
                    block = rg_ref[s, j]
                    first = s * nb + 2 * j
                    a0 = agg_ref[row * panel + first] - floor
                    a1 = agg_ref[row * panel + first + 1] - floor
                    for d in range(3):
                        keep = jnp.where(left_row, jnp.where(a0 == d, 1.0, 0.0), jnp.where(a1 == d, 1.0, 0.0))
                        keep = keep.astype(jnp.bfloat16)
                        lefts[d].append(block * jnp.concatenate([keep] * 4, axis=0))
                    for q in range(2):
                        at = (first + q) * 4
                        i0, i1, i2 = (last_smem[0, at + ca] for ca in range(3))
                        upper = jnp.where(left_half, sums[i0], turned[i1])
                        lower = jnp.where(left_half, turned[i0], sums[i1])
                        rights.append(jnp.concatenate([upper, sums[i2]], axis=1))
                        rights.append(jnp.concatenate([lower, turned[i2]], axis=1))
                lhs = jnp.concatenate([jnp.concatenate(l, axis=1) for l in lefts], axis=0)
                rhs = jnp.concatenate(rights, axis=0)
                made = jnp.dot(lhs, rhs, preferred_element_type=jnp.float32)
                total = made if total is None else total + made
            at = pl.ds(pl.multiple_of(base * 64, 64), 192)
            part[at, :] = part[at, :] + total
            return 0

        lax.fori_loop(lo, hi, body, 0)

    def arrived(offsets):
        for o in offsets:
            go_over(chip_at(o) * CORES + 1 - k).wait_recv()

    def invert():
        load_owner.wait()

        def body(s, _):
            inverse[s] = lax.fori_loop(0, n_col, lambda t, got: jnp.where(owner_ref[t] == s, t, got), 0, unroll=True)
            return 0

        lax.fori_loop(0, n_col, body, 0)

    part[...] = jnp.zeros_like(part)
    load_a.wait()
    turn(0, 32)
    run = jnp.zeros((32, 128), jnp.float32)
    groups = slots // GROUP
    done = 0

    def some(n, run):
        nonlocal done
        lo, done = done, min(done + n, groups)
        return multiply(lo, done, run) if lo < done else run

    for d in range(1, half_ring):
        for c in range(CHUNKS):
            pass_on(d, c)
            if d == 1 and c == 0:
                tables()
            elif d == 1 and c == 1:
                widen()
            elif d == 1 and c == 2:
                invert()
            elif d < half_ring - 1:
                run = some(1, run)
            else:
                run = some(2, run)
    run = some(groups, run)
    arrived([0])
    for d in range(1, half_ring - 1):
        arrived([-d, d])
    ready = 2 + 4 * (half_ring - 2)
    dense(0, ready)
    far_end()
    arrived([1 - half_ring, half_ring - 1])
    dense(ready, ready + 4)
    arrived([half_ring])
    dense(ready + 4, ready + 6)

    lane_left = lax.broadcasted_iota(jnp.int32, (32, 128), 1) < 64

    def packed(a, lo):
        top = part[a * 64 : a * 64 + 32, lo * 128 : lo * 128 + 128]
        low = part[a * 64 + 32 : a * 64 + 64, lo * 128 : lo * 128 + 128]
        return top, low

    def halves_left(top, low):
        return jnp.where(lane_left, top, jnp.concatenate([low[:, 64:128], low[:, 0:64]], axis=1))

    def halves_right(top, low):
        return jnp.where(lane_left, jnp.concatenate([top[:, 64:128], top[:, 0:64]], axis=1), low)

    first_core = k == 0
    for a in range(row_width):
        t0, l0 = packed(a, 0)
        t1, l1 = packed(a, 1)
        e0 = halves_left(t0, l0).astype(jnp.bfloat16)
        e2 = halves_left(t1, l1).astype(jnp.bfloat16)
        edge_sib[0, a] = jnp.where(first_core, e2, e0)
        edge_out[a] = jnp.where(first_core, e0, e2)

    def scopy():
        return pltpu.make_async_remote_copy(
            src_ref=edge_sib.at[0], dst_ref=edge_sib.at[1], send_sem=ssend_sem.at[0], recv_sem=srecv_sem.at[0],
            device_id=(row, sibling), device_id_type=MESH,
        )

    def ecopy(r, w):
        return pltpu.make_async_remote_copy(
            src_ref=edge_out, dst_ref=edge_in.at[row], send_sem=esend_sem.at[w], recv_sem=erecv_sem.at[row],
            device_id=(r, beside), device_id_type=MESH,
        )

    scopy().start()

    @pl.when(has_beside)
    def _():
        for w, r in enumerate(other_row + [row]):
            ecopy(r, w).start()

    @pl.when(jnp.logical_not(has_beside))
    def _():
        edge_in[...] = jnp.zeros_like(edge_in)

    for a in range(row_width):
        mid[a] = halves_right(*packed(a, 0))
    scopy().wait_recv()
    for a in range(row_width):
        mid_in[row, a] = (mid[a] + edge_sib[1, a].astype(jnp.float32)).astype(jnp.bfloat16)

    def mcopy(source, w, target):
        return pltpu.make_async_remote_copy(
            src_ref=mid_in.at[source], dst_ref=mid_in.at[source], send_sem=msend_sem.at[w], recv_sem=mrecv_sem.at[source],
            device_id=(target, me), device_id_type=MESH,
        )

    for w, o in enumerate(other_row):
        mcopy(row, w, o).start()

    @pl.when(has_beside)
    def _():
        for r in [row] + other_row:
            pltpu.make_async_remote_copy(
                src_ref=edge_out, dst_ref=edge_in.at[r], send_sem=esend_sem.at[0], recv_sem=erecv_sem.at[r],
                device_id=(r, beside), device_id_type=MESH,
            ).wait_recv()

    for o in other_row:
        mcopy(o, 0, o).wait_recv()
    panel_agg = n_col // n_row
    for a in range(n_col):
        pieces = []
        for r in range(n_row):
            at = a - r * panel_agg + 1
            if 0 <= at < row_width:
                pieces.append(mid_in[r, at].astype(jnp.float32) + edge_in[r, at].astype(jnp.float32))
        full[a] = functools.reduce(jnp.add, pieces).astype(jnp.bfloat16)

    def dcopy(s):
        return pltpu.make_async_remote_copy(
            src_ref=outgoing.at[s], dst_ref=incoming.at[me], send_sem=send_sem.at[s], recv_sem=recv2_sem.at[me],
            device_id=(row, s), device_id_type=MESH,
        )

    def post(i, _):
        s = lax.rem(me + i, n_col)
        outgoing[s] = full[inverse[s]]
        dcopy(s).start()
        return 0

    lax.fori_loop(1, n_col, post, 0)
    incoming[me] = full[inverse[me]]

    def emit(c):
        block = incoming[c].astype(jnp.float32)
        out_ref[0, c, 0:32, :] = block[:, 0:64]
        out_ref[0, c, 32:64, :] = block[:, 64:128]

    emit(me)

    for d in range(half_ring):
        for c in range(CHUNKS):
            if d < half_ring - 1 or c < half:
                go_right(shard_at(-d), c).wait_send()
                go_left(shard_at(d), (c + half) % CHUNKS).wait_send()
    for i in range(chips):
        go_over(i * CORES + k).wait_send()
    for w, o in enumerate(other_row):
        pcopy(w, o).wait_send()
        mcopy(row, w, o).wait_send()
    scopy().wait_send()

    @pl.when(has_beside)
    def _():
        for w, r in enumerate(other_row + [row]):
            ecopy(r, w).wait_send()

    def arrive(i, _):
        c = lax.rem(me + n_col - i, n_col)
        pltpu.make_async_remote_copy(
            src_ref=outgoing.at[0], dst_ref=incoming.at[c], send_sem=send_sem.at[c], recv_sem=recv2_sem.at[c],
            device_id=(row, c), device_id_type=MESH,
        ).wait_recv()
        emit(c)
        return 0

    lax.fori_loop(1, n_col, arrive, 0)

    def sent(i, _):
        dcopy(lax.rem(me + i, n_col)).wait_send()
        return 0

    lax.fori_loop(1, n_col, sent, 0)


def on_device(n_row, n_col, a_blocks, block_rows, block_cols, block_count, restrict, interp, aggregate, owner):
    vmem = pl.BlockSpec(memory_space=pltpu.VMEM)
    hbm = pl.BlockSpec(memory_space=pltpu.HBM)
    nb = restrict.shape[0]
    nj, piece = interp.shape[:2]
    slots = a_blocks.shape[2]
    agg_total = owner.shape[0]
    assert agg_total == n_col
    row_width = agg_total // n_row + 2
    bf16, f32, i32 = jnp.bfloat16, jnp.float32, jnp.int32
    chips = n_col // CORES
    panel = nb * n_col
    sized = jnp.transpose(a_blocks[0, 0], (1, 2, 0))
    dma = pltpu.SemaphoreType.DMA
    return pl.pallas_call(
        functools.partial(coarse_kernel, n_row, n_col),
        out_shape=jax.ShapeDtypeStruct((1, agg_total, 64, 64), f32),
        in_specs=[hbm] * 8,
        out_specs=vmem,
        scratch_shapes=[
            pltpu.VMEM((1, slots), i32),
            pltpu.VMEM((1, slots), i32),
            pltpu.SMEM((1, 1), i32),
            pltpu.SMEM((aggregate.shape[0],), i32),
            pltpu.SMEM((agg_total,), i32),
            pltpu.VMEM((nb, 64, 64), bf16),
            pltpu.VMEM((nj, piece, 64), bf16),
            pltpu.VMEM((64, 64, slots), bf16),
            pltpu.VMEM((n_col, nb // 2, 64, 128), bf16),
            pltpu.VMEM((n_row, nj // 2, piece, 128), bf16),
            pltpu.VMEM((slots, 32, 128), f32),
            pltpu.VMEM((nj, 128, 128), bf16),
            pltpu.VMEM((slots + 1, 32, 128), bf16),
            pltpu.VMEM((slots + 1, 32, 128), bf16),
            pltpu.VMEM((slots, 128), i32),
            pltpu.VMEM((slots, 128), i32),
            pltpu.VMEM((1, slots), i32),
            pltpu.VMEM((1, panel * 4), i32),
            pltpu.SMEM((1, slots), i32),
            pltpu.SMEM((1, panel * 4), i32),
            pltpu.VMEM((row_width * 64, 256), f32),
            pltpu.VMEM((row_width, 32, 128), bf16),
            pltpu.VMEM((2, row_width, 32, 128), bf16),
            pltpu.VMEM((n_row, row_width, 32, 128), bf16),
            pltpu.VMEM((row_width, 32, 128), f32),
            pltpu.VMEM((n_row, row_width, 32, 128), bf16),
            pltpu.VMEM((n_col, 32, 128), bf16),
            pltpu.VMEM((n_col, 32, 128), bf16),
            pltpu.VMEM((n_col, 32, 128), bf16),
            pltpu.SMEM((n_col,), i32),
            dma((8,)),
            dma((2,)),
            dma((n_col, CHUNKS)),
            dma((n_col, CHUNKS)),
            dma((n_col,)),
            dma((n_col, CHUNKS)),
            dma((n_row,)),
            dma((n_row,)),
            dma((1,)),
            dma((1,)),
            dma((n_row,)),
            dma((n_row,)),
            dma((n_row,)),
            dma((n_row,)),
            dma((n_col,)),
            dma((n_col,)),
        ],
        compiler_params=pltpu.CompilerParams(collective_id=0, has_side_effects=True, vmem_limit_bytes=60 * 2**20),
        name="coarse_operator",
    )(block_rows[0], block_cols[0], block_count, aggregate, owner, restrict, interp, sized)


def solution(mesh):
    return jax.shard_map(
        functools.partial(on_device, mesh.shape["row"], mesh.shape["col"]),
        mesh=mesh,
        in_specs=(
            P("row", "col", None, None, None),
            P("row", "col", None),
            P("row", "col", None),
            P("row", "col"),
            P(("row", "col"), None, None),
            P("col", "row", None),
            P(),
            P(),
        ),
        out_specs=P("col", None, None, None),
        check_vma=False,
    )
```

```python
import functools

import jax
import jax.numpy as jnp
from jax import lax
from jax.experimental import pallas as pl
from jax.experimental.pallas import tpu as pltpu
from jax.sharding import PartitionSpec as P

MESH = pl.DeviceIdType.MESH
CORES = 2
DEPTH = 4
CHUNKS = 4
GROUP = 64
SLOT_BITS = 9
COL_BITS = 6
KEY_SHIFT = SLOT_BITS + COL_BITS


def coarse_kernel(
    n_row, n_col, rows_hbm, cols_hbm, count_hbm, agg_hbm, owner_hbm, r_hbm, p_hbm, a_hbm, incoming,
    rows_ref, cols_ref, count_ref, agg_ref, owner_ref, r_ref, p_ref, a_ref,
    rg_ref, pg_ref, flat, wide, sums, turned, v_col, rank_col, v_tab, last_tab, v_smem, last_smem, keep_ref, part,
    edge_out, edge_sib, edge_in, mid, mid_in, full, outgoing, inverse,
    load_sem, tab_sem, right_sem, left_sem, sib_sem, recv_sem, psend_sem, precv_sem,
    ssend_sem, srecv_sem, esend_sem, erecv_sem, msend_sem, mrecv_sem, send_sem, recv2_sem,
):
    width = n_col // (CORES * DEPTH)
    chips = n_col // CORES
    half_ring = chips // 2
    me = lax.axis_index("col")
    row = lax.axis_index("row")
    z = me // (width * CORES)
    x = lax.rem(me // CORES, width)
    k = lax.rem(me, CORES)
    sibling = me + 1 - 2 * k
    beside = me - 1 + 2 * k
    has_beside = (beside >= 0) & (beside < n_col)
    other_row = [lax.rem(row + d, n_row) for d in range(1, n_row)]

    back = DEPTH - 1 - z
    spot = jnp.where(
        x == 0, z, DEPTH + back * (width - 1) + jnp.where(lax.rem(back, 2) == 0, x - 1, width - 1 - x)
    )

    def chip_at(offset):
        s = lax.rem(spot + offset + chips, chips)
        b = (s - DEPTH) // (width - 1)
        i = lax.rem(s - DEPTH, width - 1)
        far = (DEPTH - 1 - b) * width + jnp.where(lax.rem(b, 2) == 0, i + 1, width - 1 - i)
        return jnp.where(s < DEPTH, s * width, far)

    def shard_at(offset):
        return chip_at(offset) * CORES + k

    right = shard_at(1)
    left = shard_at(-1)

    nb = r_ref.shape[0]
    tiles = nb // 2
    half_p = p_ref.shape[0] // 2
    piece = p_ref.shape[1]
    nj = p_ref.shape[0]
    slots = a_ref.shape[2]
    panel = nb * n_col
    per_agg = agg_ref.shape[0] // n_col
    row_width = part.shape[0] // 64

    loads = [
        pltpu.make_async_copy(src, dst, load_sem.at[i])
        for i, (src, dst) in enumerate(
            [
                (r_hbm, r_ref), (p_hbm, p_ref), (rows_hbm, rows_ref), (cols_hbm, cols_ref), (count_hbm, count_ref),
                (agg_hbm, agg_ref), (owner_hbm, owner_ref), (a_hbm, a_ref),
            ]
        )
    ]
    for load in loads:
        load.start()
    load_r, load_p, load_rows, load_cols, load_count, load_agg, load_owner, load_a = loads

    barrier = pltpu.get_barrier_semaphore()

    def greet(dev):
        pl.semaphore_signal(barrier, inc=1, device_id=dev, device_id_type=MESH)

    def greet_row(i, _):
        greet((row, lax.rem(me + i, n_col)))
        return 0

    lax.fori_loop(1, n_col, greet_row, 0)
    for o in other_row:
        greet((o, me))

    @pl.when(has_beside)
    def _():
        for o in other_row:
            greet((o, beside))

    tile_ends = [(s, min(s + 128, slots)) for s in range(0, slots, 128)]

    table_copies = [
        pltpu.make_async_copy(v_tab, v_smem, tab_sem.at[0]), pltpu.make_async_copy(last_tab, last_smem, tab_sem.at[1])
    ]

    def tables():
        load_rows.wait()
        load_cols.wait()
        load_count.wait()
        load_agg.wait()
        cols = cols_ref[...]
        off = jnp.zeros_like(cols)
        for j in range(nj):
            off = jnp.where(cols == j, agg_ref[me * nj + j] - (me - 1), off)
        slot = lax.broadcasted_iota(jnp.int32, (1, slots), 1)
        key = jnp.where(slot < count_ref[0, 0], rows_ref[...] * 4 + off, panel * 4)
        v = (key * 2**COL_BITS + cols) * 2**SLOT_BITS + slot
        for s, e in tile_ends:
            v_col[s:e, :] = jnp.broadcast_to(v[:, s:e], (128, e - s)).T
        for s, e in tile_ends:
            below = (v_col[:, 0 : e - s] < v[:, s:e]).astype(jnp.int32)
            rank = jnp.sum(below, axis=0, keepdims=True)
            rank_col[s:e, :] = jnp.broadcast_to(rank, (128, e - s)).T
        for s, e in tile_ends:
            place = lax.broadcasted_iota(jnp.int32, (1, e - s), 1) + s
            hit = rank_col[:, 0 : e - s] == place
            v_tab[:, s:e] = jnp.sum(jnp.where(hit, v_col[:, 0 : e - s], 0), axis=0, keepdims=True)
        for s in range(0, panel * 4, 128):
            place = lax.broadcasted_iota(jnp.int32, (1, 128), 1) + s
            keys = v_col[...] >> KEY_SHIFT
            upto = jnp.sum((keys <= place).astype(jnp.int32), axis=0, keepdims=True)
            under = jnp.sum((keys < place).astype(jnp.int32), axis=0, keepdims=True)
            last_tab[:, s : s + 128] = jnp.where(upto > under, upto, 0)
        for c in table_copies:
            c.start()

    tables()
    load_r.wait()
    for j in range(tiles):
        rg_ref[me, j] = jnp.concatenate([r_ref[2 * j], r_ref[2 * j + 1]], axis=1)
    pl.semaphore_wait(barrier, n_col - 1 + len(other_row) + jnp.where(has_beside, len(other_row), 0))

    size = tiles // CHUNKS
    half = CHUNKS // 2

    def ring(shard, c, sem, target):
        piece_of = rg_ref.at[shard, pl.ds(c * size, size)]
        return pltpu.make_async_remote_copy(
            src_ref=piece_of, dst_ref=piece_of, send_sem=sem.at[shard, c], recv_sem=recv_sem.at[shard, c],
            device_id=(row, target), device_id_type=MESH,
        )

    def go_right(shard, c):
        return ring(shard, c, right_sem, right)

    def go_left(shard, c):
        return ring(shard, c, left_sem, left)

    def go_over(shard):
        return pltpu.make_async_remote_copy(
            src_ref=rg_ref.at[shard], dst_ref=rg_ref.at[shard], send_sem=sib_sem.at[shard], recv_sem=recv_sem.at[shard, 0],
            device_id=(row, sibling), device_id_type=MESH,
        )

    def pcopy(way, target):
        return pltpu.make_async_remote_copy(
            src_ref=pg_ref.at[row], dst_ref=pg_ref.at[row], send_sem=psend_sem.at[way], recv_sem=precv_sem.at[row],
            device_id=(target, me), device_id_type=MESH,
        )

    for c in range(CHUNKS):
        go_right(me, c).start()
        go_left(me, (c + half) % CHUNKS).start()
    go_over(me).start()
    load_p.wait()
    for j in range(half_p):
        pg_ref[row, j, :, 0:64] = p_ref[j]
        pg_ref[row, j, :, 64:128] = p_ref[j + half_p]
    for w, o in enumerate(other_row):
        pcopy(w, o).start()

    def pass_on(d, c):
        back_c = (c + half) % CHUNKS
        onward = d < half_ring - 1 or c < half
        s = shard_at(-d)
        go_right(s, c).wait_recv()
        if onward:
            go_right(s, c).start()
        s = shard_at(d)
        go_left(s, back_c).wait_recv()
        if onward:
            go_left(s, back_c).start()
        if c == CHUNKS - 1:
            go_over(shard_at(-d)).start()
            go_over(shard_at(d)).start()

    def far_end():
        s = shard_at(half_ring)
        for c in range(CHUNKS):
            go_right(s, c).wait_recv()
        go_over(s).start()

    def turn(lo, hi):
        def body(i, _):
            for s, e in tile_ends:
                tall = jnp.concatenate([a_ref[i, :, s:e], a_ref[i + 32, :, s:e]], axis=0)
                flat[s:e, i, :] = tall.T.astype(jnp.float32)
            return 0

        lax.fori_loop(lo, hi, body, 0)

    def widen():
        for o in other_row:
            pltpu.make_async_remote_copy(
                src_ref=pg_ref.at[o], dst_ref=pg_ref.at[o], send_sem=psend_sem.at[0], recv_sem=precv_sem.at[o],
                device_id=(o, me), device_id_type=MESH,
            ).wait_recv()
        wide[...] = jnp.zeros_like(wide)

        def body(j, _):
            for r in range(n_row):
                lo, hi = r * piece, (r + 1) * piece
                both = pg_ref[r, j]
                wide[j, lo:hi, 0:64] = both[:, 0:64]
                wide[j, 64 + lo : 64 + hi, 64:128] = both[:, 0:64]
                wide[j + half_p, lo:hi, 0:64] = both[:, 64:128]
                wide[j + half_p, 64 + lo : 64 + hi, 64:128] = both[:, 64:128]
            return 0

        lax.fori_loop(0, half_p, body, 0, unroll=2)
        sums[0] = jnp.zeros((32, 128), jnp.bfloat16)
        turned[0] = jnp.zeros((32, 128), jnp.bfloat16)

    def multiply(lo, hi, run):
        def body(g, run):
            base = g * GROUP
            made = []
            for u in range(GROUP):
                v = v_smem[0, base + u]
                left_side = flat[v & (2**SLOT_BITS - 1)].astype(jnp.bfloat16)
                right_side = wide[(v >> SLOT_BITS) & (2**COL_BITS - 1)]
                product = jnp.dot(left_side, right_side, preferred_element_type=jnp.float32).astype(jnp.bfloat16)
                made.append(product)
            before = v_smem[0, jnp.maximum(base - 1, 0)] >> KEY_SHIFT
            for u in range(GROUP):
                now = v_smem[0, base + u] >> KEY_SHIFT
                run = run * jnp.where(now == before, 1.0, 0.0) + made[u].astype(jnp.float32)
                before = now
                both = run.astype(jnp.bfloat16)
                sums[base + u + 1] = both
                turned[base + u + 1] = jnp.concatenate([both[:, 64:128], both[:, 0:64]], axis=1)
            return run

        return lax.fori_loop(lo, hi, body, run)

    left_half = lax.broadcasted_iota(jnp.int32, (32, 128), 1) < 64
    left_row = lax.broadcasted_iota(jnp.int32, (16, 128), 1) < 64

    def masks():
        def body(s, _):
            floor = row * (n_col // n_row) + s * nb // per_agg - 1
            for j in range(tiles):
                first = row * panel + s * nb + 2 * j
                a0 = agg_ref[first] - floor
                a1 = agg_ref[first + 1] - floor
                for d in range(3):
                    keep = jnp.where(left_row, jnp.where(a0 == d, 1.0, 0.0), jnp.where(a1 == d, 1.0, 0.0))
                    keep_ref[s * tiles + j, d] = keep.astype(jnp.bfloat16)
            return 0

        lax.fori_loop(0, n_col, body, 0)

    def dense(lo, hi):
        def body(i, _):
            step = (i + 1) // 2
            chip = chip_at(jnp.where(lax.rem(i, 2) == 0, step, -step))
            base = chip * CORES * nb // per_agg
            total = None
            for t in range(CORES * tiles // 2):
                lefts = [[], [], []]
                rights = []
                for h in range(2):
                    s = chip * CORES + (2 * t + h) // tiles
                    j = (2 * t + h) % tiles
                    block = rg_ref[s, j]
                    for d in range(3):
                        lefts[d].append(block * jnp.concatenate([keep_ref[s * tiles + j, d]] * 4, axis=0))
                    for q in range(2):
                        at = (s * nb + 2 * j + q) * 4
                        i0, i1, i2 = (last_smem[0, at + ca] for ca in range(3))
                        upper = jnp.where(left_half, sums[i0], turned[i1])
                        lower = jnp.where(left_half, turned[i0], sums[i1])
                        rights.append(jnp.concatenate([upper, sums[i2]], axis=1))
                        rights.append(jnp.concatenate([lower, turned[i2]], axis=1))
                lhs = jnp.concatenate([jnp.concatenate(l, axis=1) for l in lefts], axis=0)
                rhs = jnp.concatenate(rights, axis=0)
                made = jnp.dot(lhs, rhs, preferred_element_type=jnp.float32)
                total = made if total is None else total + made
            at = pl.ds(pl.multiple_of(base * 64, 64), 192)
            part[at, :] = part[at, :] + total
            return 0

        lax.fori_loop(lo, hi, body, 0)

    def arrived(offsets):
        for o in offsets:
            go_over(chip_at(o) * CORES + 1 - k).wait_recv()

    def invert():
        load_owner.wait()

        def body(s, _):
            inverse[s] = lax.fori_loop(0, n_col, lambda t, got: jnp.where(owner_ref[t] == s, t, got), 0, unroll=True)
            return 0

        lax.fori_loop(0, n_col, body, 0)

    part[...] = jnp.zeros_like(part)
    load_a.wait()
    turn(0, 32)
    for c in table_copies:
        c.wait()
    run = jnp.zeros((32, 128), jnp.float32)
    groups = slots // GROUP
    done = 0
    cooked = 0
    pending = [0]
    for d in range(1, half_ring):
        for c in range(CHUNKS):
            pass_on(d, c)
            if c == CHUNKS - 1:
                pending += [-d, d]
            spot_no = (d - 1) * CHUNKS + c
            if spot_no == 0:
                widen()
            elif spot_no == 1:
                masks()
                invert()
            elif done < groups:
                run = multiply(done, done + 1, run)
                done += 1
            elif len(pending) > 2 + 2 * (c == CHUNKS - 1):
                arrived(pending[:1])
                pending = pending[1:]
                dense(cooked, cooked + 1)
                cooked += 1
    if done < groups:
        run = multiply(done, groups, run)
    if pending[:-2]:
        arrived(pending[:-2])
        dense(cooked, cooked + len(pending) - 2)
        cooked += len(pending) - 2
    far_end()
    arrived(pending[-2:])
    dense(cooked, cooked + 2)
    arrived([half_ring])
    dense(cooked + 2, cooked + 3)

    lane_left = lax.broadcasted_iota(jnp.int32, (32, 128), 1) < 64

    def packed(a, lo):
        top = part[a * 64 : a * 64 + 32, lo * 128 : lo * 128 + 128]
        low = part[a * 64 + 32 : a * 64 + 64, lo * 128 : lo * 128 + 128]
        return top, low

    def halves_left(top, low):
        return jnp.where(lane_left, top, jnp.concatenate([low[:, 64:128], low[:, 0:64]], axis=1))

    def halves_right(top, low):
        return jnp.where(lane_left, jnp.concatenate([top[:, 64:128], top[:, 0:64]], axis=1), low)

    first_core = k == 0
    for a in range(row_width):
        t0, l0 = packed(a, 0)
        t1, l1 = packed(a, 1)
        e0 = halves_left(t0, l0).astype(jnp.bfloat16)
        e2 = halves_left(t1, l1).astype(jnp.bfloat16)
        edge_sib[0, a] = jnp.where(first_core, e2, e0)
        edge_out[a] = jnp.where(first_core, e0, e2)

    def scopy():
        return pltpu.make_async_remote_copy(
            src_ref=edge_sib.at[0], dst_ref=edge_sib.at[1], send_sem=ssend_sem.at[0], recv_sem=srecv_sem.at[0],
            device_id=(row, sibling), device_id_type=MESH,
        )

    def ecopy(r, w):
        return pltpu.make_async_remote_copy(
            src_ref=edge_out, dst_ref=edge_in.at[row], send_sem=esend_sem.at[w], recv_sem=erecv_sem.at[row],
            device_id=(r, beside), device_id_type=MESH,
        )

    scopy().start()

    @pl.when(has_beside)
    def _():
        for w, r in enumerate(other_row + [row]):
            ecopy(r, w).start()

    @pl.when(jnp.logical_not(has_beside))
    def _():
        edge_in[...] = jnp.zeros_like(edge_in)

    for a in range(row_width):
        mid[a] = halves_right(*packed(a, 0))
    scopy().wait_recv()
    for a in range(row_width):
        mid_in[row, a] = (mid[a] + edge_sib[1, a].astype(jnp.float32)).astype(jnp.bfloat16)

    def mcopy(source, w, target):
        return pltpu.make_async_remote_copy(
            src_ref=mid_in.at[source], dst_ref=mid_in.at[source], send_sem=msend_sem.at[w], recv_sem=mrecv_sem.at[source],
            device_id=(target, me), device_id_type=MESH,
        )

    for w, o in enumerate(other_row):
        mcopy(row, w, o).start()

    @pl.when(has_beside)
    def _():
        for r in [row] + other_row:
            pltpu.make_async_remote_copy(
                src_ref=edge_out, dst_ref=edge_in.at[r], send_sem=esend_sem.at[0], recv_sem=erecv_sem.at[r],
                device_id=(r, beside), device_id_type=MESH,
            ).wait_recv()

    for o in other_row:
        mcopy(o, 0, o).wait_recv()
    panel_agg = n_col // n_row
    for a in range(n_col):
        pieces = []
        for r in range(n_row):
            at = a - r * panel_agg + 1
            if 0 <= at < row_width:
                pieces.append(mid_in[r, at].astype(jnp.float32) + edge_in[r, at].astype(jnp.float32))
        full[a] = functools.reduce(jnp.add, pieces).astype(jnp.bfloat16)

    def dcopy(s):
        return pltpu.make_async_remote_copy(
            src_ref=outgoing.at[s], dst_ref=incoming.at[me], send_sem=send_sem.at[s], recv_sem=recv2_sem.at[me],
            device_id=(row, s), device_id_type=MESH,
        )

    def post(i, _):
        s = lax.rem(me + i, n_col)
        outgoing[s] = full[inverse[s]]
        dcopy(s).start()
        return 0

    lax.fori_loop(1, n_col, post, 0)
    incoming[me] = full[inverse[me]]

    for d in range(half_ring):
        for c in range(CHUNKS):
            if d < half_ring - 1 or c < half:
                go_right(shard_at(-d), c).wait_send()
                go_left(shard_at(d), (c + half) % CHUNKS).wait_send()
    for i in range(chips):
        go_over(i * CORES + k).wait_send()
    for w, o in enumerate(other_row):
        pcopy(w, o).wait_send()
        mcopy(row, w, o).wait_send()
    scopy().wait_send()

    @pl.when(has_beside)
    def _():
        for w, r in enumerate(other_row + [row]):
            ecopy(r, w).wait_send()

    def arrive(i, _):
        c = lax.rem(me + n_col - i, n_col)
        pltpu.make_async_remote_copy(
            src_ref=outgoing.at[0], dst_ref=incoming.at[c], send_sem=send_sem.at[c], recv_sem=recv2_sem.at[c],
            device_id=(row, c), device_id_type=MESH,
        ).wait_recv()
        return 0

    lax.fori_loop(1, n_col, arrive, 0)

    def sent(i, _):
        dcopy(lax.rem(me + i, n_col)).wait_send()
        return 0

    lax.fori_loop(1, n_col, sent, 0)


def on_device(n_row, n_col, a_blocks, block_rows, block_cols, block_count, restrict, interp, aggregate, owner):
    vmem = pl.BlockSpec(memory_space=pltpu.VMEM)
    hbm = pl.BlockSpec(memory_space=pltpu.HBM)
    nb = restrict.shape[0]
    nj, piece = interp.shape[:2]
    slots = a_blocks.shape[2]
    agg_total = owner.shape[0]
    assert agg_total == n_col
    row_width = agg_total // n_row + 2
    bf16, f32, i32 = jnp.bfloat16, jnp.float32, jnp.int32
    chips = n_col // CORES
    panel = nb * n_col
    sized = jnp.transpose(a_blocks[0, 0], (1, 2, 0))
    dma = pltpu.SemaphoreType.DMA
    blocks = pl.pallas_call(
        functools.partial(coarse_kernel, n_row, n_col),
        out_shape=jax.ShapeDtypeStruct((n_col, 32, 128), bf16),
        in_specs=[hbm] * 8,
        out_specs=vmem,
        scratch_shapes=[
            pltpu.VMEM((1, slots), i32),
            pltpu.VMEM((1, slots), i32),
            pltpu.SMEM((1, 1), i32),
            pltpu.SMEM((aggregate.shape[0],), i32),
            pltpu.SMEM((agg_total,), i32),
            pltpu.VMEM((nb, 64, 64), bf16),
            pltpu.VMEM((nj, piece, 64), bf16),
            pltpu.VMEM((64, 64, slots), bf16),
            pltpu.VMEM((n_col, nb // 2, 64, 128), bf16),
            pltpu.VMEM((n_row, nj // 2, piece, 128), bf16),
            pltpu.VMEM((slots, 32, 128), f32),
            pltpu.VMEM((nj, 128, 128), bf16),
            pltpu.VMEM((slots + 1, 32, 128), bf16),
            pltpu.VMEM((slots + 1, 32, 128), bf16),
            pltpu.VMEM((slots, 128), i32),
            pltpu.VMEM((slots, 128), i32),
            pltpu.VMEM((1, slots), i32),
            pltpu.VMEM((1, panel * 4), i32),
            pltpu.SMEM((1, slots), i32),
            pltpu.SMEM((1, panel * 4), i32),
            pltpu.VMEM((panel // 2, 3, 16, 128), bf16),
            pltpu.VMEM((row_width * 64, 256), f32),
            pltpu.VMEM((row_width, 32, 128), bf16),
            pltpu.VMEM((2, row_width, 32, 128), bf16),
            pltpu.VMEM((n_row, row_width, 32, 128), bf16),
            pltpu.VMEM((row_width, 32, 128), f32),
            pltpu.VMEM((n_row, row_width, 32, 128), bf16),
            pltpu.VMEM((n_col, 32, 128), bf16),
            pltpu.VMEM((n_col, 32, 128), bf16),
            pltpu.SMEM((n_col,), i32),
            dma((8,)),
            dma((2,)),
            dma((n_col, CHUNKS)),
            dma((n_col, CHUNKS)),
            dma((n_col,)),
            dma((n_col, CHUNKS)),
            dma((n_row,)),
            dma((n_row,)),
            dma((1,)),
            dma((1,)),
            dma((n_row,)),
            dma((n_row,)),
            dma((n_row,)),
            dma((n_row,)),
            dma((n_col,)),
            dma((n_col,)),
        ],
        compiler_params=pltpu.CompilerParams(collective_id=0, has_side_effects=True, vmem_limit_bytes=60 * 2**20),
        name="coarse_operator",
    )(block_rows[0], block_cols[0], block_count, aggregate, owner, restrict, interp, sized)
    return jnp.concatenate([blocks[:, :, :64], blocks[:, :, 64:]], axis=1).astype(f32)[None]


def solution(mesh):
    return jax.shard_map(
        functools.partial(on_device, mesh.shape["row"], mesh.shape["col"]),
        mesh=mesh,
        in_specs=(
            P("row", "col", None, None, None),
            P("row", "col", None),
            P("row", "col", None),
            P("row", "col"),
            P(("row", "col"), None, None),
            P("col", "row", None),
            P(),
            P(),
        ),
        out_specs=P("col", None, None, None),
        check_vma=False,
    )
```

```python
import functools

import jax
import jax.numpy as jnp
from jax import lax
from jax.experimental import pallas as pl
from jax.experimental.pallas import tpu as pltpu
from jax.sharding import PartitionSpec as P

MESH = pl.DeviceIdType.MESH
CORES = 2
DEPTH = 4
CHUNKS = 4
GROUP = 64
SLOT_BITS = 9
COL_BITS = 6
KEY_SHIFT = SLOT_BITS + COL_BITS


def coarse_kernel(
    n_row, n_col, rows_hbm, cols_hbm, count_hbm, agg_hbm, owner_hbm, r_hbm, p_hbm, a_hbm, incoming,
    rows_ref, cols_ref, count_ref, agg_ref, owner_ref, r_ref, p_ref, a_ref,
    rg_ref, pg_ref, flat, wide, sums, turned, v_col, rank_col, v_tab, last_tab, v_smem, last_smem, keep_ref, part,
    edge_out, edge_sib, edge_in, mid_in, full, outgoing, inverse,
    load_sem, tab_sem, right_sem, left_sem, sib_sem, recv_sem, psend_sem, precv_sem,
    ssend_sem, srecv_sem, esend_sem, erecv_sem, msend_sem, mrecv_sem, send_sem, recv2_sem,
):
    width = n_col // (CORES * DEPTH)
    chips = n_col // CORES
    half_ring = chips // 2
    me = lax.axis_index("col")
    row = lax.axis_index("row")
    z = me // (width * CORES)
    x = lax.rem(me // CORES, width)
    k = lax.rem(me, CORES)
    sibling = me + 1 - 2 * k
    beside = me - 1 + 2 * k
    has_beside = (beside >= 0) & (beside < n_col)
    other_row = [lax.rem(row + d, n_row) for d in range(1, n_row)]

    def spot_of(zz, xx):
        back = DEPTH - 1 - zz
        return jnp.where(
            xx == 0, zz, DEPTH + back * (width - 1) + jnp.where(lax.rem(back, 2) == 0, xx - 1, width - 1 - xx)
        )

    spot = spot_of(z, x)

    def chip_on(s):
        s = lax.rem(s + chips, chips)
        b = (s - DEPTH) // (width - 1)
        i = lax.rem(s - DEPTH, width - 1)
        far = (DEPTH - 1 - b) * width + jnp.where(lax.rem(b, 2) == 0, i + 1, width - 1 - i)
        return jnp.where(s < DEPTH, s * width, far)

    def chip_at(offset):
        return chip_on(spot + offset)

    def shard_at(offset):
        return chip_at(offset) * CORES + k

    right = shard_at(1)
    left = shard_at(-1)

    nb = r_ref.shape[0]
    tiles = nb // 2
    half_p = p_ref.shape[0] // 2
    piece = p_ref.shape[1]
    nj = p_ref.shape[0]
    slots = a_ref.shape[2]
    panel = nb * n_col
    per_agg = agg_ref.shape[0] // n_col
    row_width = part.shape[0] // 64

    loads = [
        pltpu.make_async_copy(src, dst, load_sem.at[i])
        for i, (src, dst) in enumerate(
            [
                (r_hbm, r_ref), (p_hbm, p_ref), (rows_hbm, rows_ref), (cols_hbm, cols_ref), (count_hbm, count_ref),
                (agg_hbm, agg_ref), (owner_hbm, owner_ref), (a_hbm, a_ref),
            ]
        )
    ]
    for load in loads:
        load.start()
    load_r, load_p, load_rows, load_cols, load_count, load_agg, load_owner, load_a = loads

    barrier = pltpu.get_barrier_semaphore()

    def greet(dev):
        pl.semaphore_signal(barrier, inc=1, device_id=dev, device_id_type=MESH)

    for near in (right, left, sibling):
        greet((row, near))
    for o in other_row:
        greet((o, me))

    @pl.when(has_beside)
    def _():
        for o in other_row:
            greet((o, beside))

    tile_ends = [(s, min(s + 128, slots)) for s in range(0, slots, 128)]

    table_copies = [
        pltpu.make_async_copy(v_tab, v_smem, tab_sem.at[0]), pltpu.make_async_copy(last_tab, last_smem, tab_sem.at[1])
    ]

    def tables():
        load_rows.wait()
        load_cols.wait()
        load_count.wait()
        load_agg.wait()
        cols = cols_ref[...]
        off = jnp.zeros_like(cols)
        for j in range(nj):
            off = jnp.where(cols == j, agg_ref[me * nj + j] - (me - 1), off)
        slot = lax.broadcasted_iota(jnp.int32, (1, slots), 1)
        key = jnp.where(slot < count_ref[0, 0], rows_ref[...] * 4 + off, panel * 4)
        v = (key * 2**COL_BITS + cols) * 2**SLOT_BITS + slot
        for s, e in tile_ends:
            v_col[s:e, :] = jnp.broadcast_to(v[:, s:e], (128, e - s)).T
        for s, e in tile_ends:
            below = (v_col[:, 0 : e - s] < v[:, s:e]).astype(jnp.int32)
            rank = jnp.sum(below, axis=0, keepdims=True)
            rank_col[s:e, :] = jnp.broadcast_to(rank, (128, e - s)).T
        for s, e in tile_ends:
            place = lax.broadcasted_iota(jnp.int32, (1, e - s), 1) + s
            hit = rank_col[:, 0 : e - s] == place
            v_tab[:, s:e] = jnp.sum(jnp.where(hit, v_col[:, 0 : e - s], 0), axis=0, keepdims=True)
        for s in range(0, panel * 4, 128):
            place = lax.broadcasted_iota(jnp.int32, (1, 128), 1) + s
            keys = v_col[...] >> KEY_SHIFT
            upto = jnp.sum((keys <= place).astype(jnp.int32), axis=0, keepdims=True)
            under = jnp.sum((keys < place).astype(jnp.int32), axis=0, keepdims=True)
            last_tab[:, s : s + 128] = jnp.where(upto > under, upto, 0)
        for c in table_copies:
            c.start()

    load_r.wait()
    for j in range(tiles):
        rg_ref[me, j] = jnp.concatenate([r_ref[2 * j], r_ref[2 * j + 1]], axis=1)
    pl.semaphore_wait(barrier, 3 + len(other_row) + jnp.where(has_beside, len(other_row), 0))

    size = tiles // CHUNKS
    half = CHUNKS // 2

    def ring(shard, c, sem, target):
        piece_of = rg_ref.at[shard, pl.ds(c * size, size)]
        return pltpu.make_async_remote_copy(
            src_ref=piece_of, dst_ref=piece_of, send_sem=sem.at[shard, c], recv_sem=recv_sem.at[shard, c],
            device_id=(row, target), device_id_type=MESH,
        )

    def go_right(shard, c):
        return ring(shard, c, right_sem, right)

    def go_left(shard, c):
        return ring(shard, c, left_sem, left)

    def go_over(shard):
        return pltpu.make_async_remote_copy(
            src_ref=rg_ref.at[shard], dst_ref=rg_ref.at[shard], send_sem=sib_sem.at[shard], recv_sem=recv_sem.at[shard, 0],
            device_id=(row, sibling), device_id_type=MESH,
        )

    def pcopy(way, target):
        return pltpu.make_async_remote_copy(
            src_ref=pg_ref.at[row], dst_ref=pg_ref.at[row], send_sem=psend_sem.at[way], recv_sem=precv_sem.at[row],
            device_id=(target, me), device_id_type=MESH,
        )

    for c in range(CHUNKS):
        go_right(me, c).start()
        go_left(me, (c + half) % CHUNKS).start()
    go_over(me).start()
    load_p.wait()
    for j in range(half_p):
        pg_ref[row, j, :, 0:64] = p_ref[j]
        pg_ref[row, j, :, 64:128] = p_ref[j + half_p]
    for w, o in enumerate(other_row):
        pcopy(w, o).start()

    def pass_on(d, c):
        back_c = (c + half) % CHUNKS
        onward = d < half_ring - 1 or c < half
        s = shard_at(-d)
        go_right(s, c).wait_recv()
        if onward:
            go_right(s, c).start()
        s = shard_at(d)
        go_left(s, back_c).wait_recv()
        if onward:
            go_left(s, back_c).start()
        if c == CHUNKS - 1:
            go_over(shard_at(-d)).start()
            go_over(shard_at(d)).start()

    def far_end():
        s = shard_at(half_ring)
        for c in range(CHUNKS):
            go_right(s, c).wait_recv()
        go_over(s).start()

    def turn(lo, hi):
        def body(i, _):
            for s, e in tile_ends:
                tall = jnp.concatenate([a_ref[i, :, s:e], a_ref[i + 32, :, s:e]], axis=0)
                flat[s:e, i, :] = tall.T.astype(jnp.float32)
            return 0

        lax.fori_loop(lo, hi, body, 0)

    def widen():
        for o in other_row:
            pltpu.make_async_remote_copy(
                src_ref=pg_ref.at[o], dst_ref=pg_ref.at[o], send_sem=psend_sem.at[0], recv_sem=precv_sem.at[o],
                device_id=(o, me), device_id_type=MESH,
            ).wait_recv()
        wide[...] = jnp.zeros_like(wide)

        def body(j, _):
            for r in range(n_row):
                lo, hi = r * piece, (r + 1) * piece
                both = pg_ref[r, j]
                wide[j, lo:hi, 0:64] = both[:, 0:64]
                wide[j, 64 + lo : 64 + hi, 64:128] = both[:, 0:64]
                wide[j + half_p, lo:hi, 0:64] = both[:, 64:128]
                wide[j + half_p, 64 + lo : 64 + hi, 64:128] = both[:, 64:128]
            return 0

        lax.fori_loop(0, half_p, body, 0, unroll=2)
        sums[0] = jnp.zeros((32, 128), jnp.bfloat16)
        turned[0] = jnp.zeros((32, 128), jnp.bfloat16)

    def multiply(lo, hi, run):
        def body(g, run):
            base = g * GROUP
            made = []
            for u in range(GROUP):
                v = v_smem[0, base + u]
                left_side = flat[v & (2**SLOT_BITS - 1)].astype(jnp.bfloat16)
                right_side = wide[(v >> SLOT_BITS) & (2**COL_BITS - 1)]
                product = jnp.dot(left_side, right_side, preferred_element_type=jnp.float32).astype(jnp.bfloat16)
                made.append(product)
            before = v_smem[0, jnp.maximum(base - 1, 0)] >> KEY_SHIFT
            for u in range(GROUP):
                now = v_smem[0, base + u] >> KEY_SHIFT
                run = run * jnp.where(now == before, 1.0, 0.0) + made[u].astype(jnp.float32)
                before = now
                both = run.astype(jnp.bfloat16)
                sums[base + u + 1] = both
                turned[base + u + 1] = jnp.concatenate([both[:, 64:128], both[:, 0:64]], axis=1)
            return run

        return lax.fori_loop(lo, hi, body, run)

    left_half = lax.broadcasted_iota(jnp.int32, (32, 128), 1) < 64
    left_row = lax.broadcasted_iota(jnp.int32, (16, 128), 1) < 64

    def masks():
        def body(s, _):
            floor = row * (n_col // n_row) + s * nb // per_agg - 1
            for j in range(tiles):
                first = row * panel + s * nb + 2 * j
                a0 = agg_ref[first] - floor
                a1 = agg_ref[first + 1] - floor
                for d in range(3):
                    keep = jnp.where(left_row, jnp.where(a0 == d, 1.0, 0.0), jnp.where(a1 == d, 1.0, 0.0))
                    keep_ref[s * tiles + j, d] = keep.astype(jnp.bfloat16)
            return 0

        lax.fori_loop(0, n_col, body, 0)

    def dense(lo, hi):
        def body(i, _):
            step = (i + 1) // 2
            chip = chip_at(jnp.where(lax.rem(i, 2) == 0, step, -step))
            base = chip * CORES * nb // per_agg
            total = None
            for t in range(CORES * tiles // 2):
                lefts = [[], [], []]
                rights = []
                for h in range(2):
                    s = chip * CORES + (2 * t + h) // tiles
                    j = (2 * t + h) % tiles
                    block = rg_ref[s, j]
                    for d in range(3):
                        lefts[d].append(block * jnp.concatenate([keep_ref[s * tiles + j, d]] * 4, axis=0))
                    for q in range(2):
                        at = (s * nb + 2 * j + q) * 4
                        i0, i1, i2 = (last_smem[0, at + ca] for ca in range(3))
                        upper = jnp.where(left_half, sums[i0], turned[i1])
                        lower = jnp.where(left_half, turned[i0], sums[i1])
                        rights.append(jnp.concatenate([upper, sums[i2]], axis=1))
                        rights.append(jnp.concatenate([lower, turned[i2]], axis=1))
                lhs = jnp.concatenate([jnp.concatenate(l, axis=1) for l in lefts], axis=0)
                rhs = jnp.concatenate(rights, axis=0)
                made = jnp.dot(lhs, rhs, preferred_element_type=jnp.float32)
                total = made if total is None else total + made
            at = pl.ds(pl.multiple_of(base * 64, 64), 192)
            part[at, :] = part[at, :] + total
            return 0

        lax.fori_loop(lo, hi, body, 0)

    def arrived(offsets):
        for o in offsets:
            go_over(chip_at(o) * CORES + 1 - k).wait_recv()

    def invert():
        load_owner.wait()

        def body(s, _):
            inverse[s] = lax.fori_loop(0, n_col, lambda t, got: jnp.where(owner_ref[t] == s, t, got), 0, unroll=True)
            return 0

        lax.fori_loop(0, n_col, body, 0)

    part[...] = jnp.zeros_like(part)
    load_a.wait()
    turn(0, 20)
    run = jnp.zeros((32, 128), jnp.float32)
    groups = slots // GROUP
    done = 0
    cooked = 0
    pending = [0]
    for d in range(1, half_ring):
        for c in range(CHUNKS):
            pass_on(d, c)
            if c == CHUNKS - 1:
                pending += [-d, d]
            spot_no = (d - 1) * CHUNKS + c
            if spot_no == 0:
                turn(20, 28)
            elif spot_no == 1:
                turn(28, 32)
                widen()
            elif spot_no == 2:
                tables()
            elif spot_no == 3:
                masks()
                invert()
                for t in table_copies:
                    t.wait()
            elif done < groups:
                run = multiply(done, done + 1, run)
                done += 1
            elif len(pending) > 2 + 2 * (c == CHUNKS - 1):
                arrived(pending[:1])
                pending = pending[1:]
                dense(cooked, cooked + 1)
                cooked += 1
    if done < groups:
        run = multiply(done, groups, run)
    if pending[:-2]:
        arrived(pending[:-2])
        dense(cooked, cooked + len(pending) - 2)
        cooked += len(pending) - 2
    far_end()
    arrived(pending[-2:])
    dense(cooked, cooked + 2)

    lane_left = lax.broadcasted_iota(jnp.int32, (32, 128), 1) < 64
    first_core = k == 0
    early = row_width - 3

    def after_last(zz, xx):
        return chip_on(spot_of(zz, xx) + half_ring) * CORES * nb // per_agg + 3

    first_row = after_last(z, x)
    first_beside = after_last(beside // (width * CORES), lax.rem(beside // CORES, width))

    def halves(i, tile, lead):
        at = lax.rem(first_row + i, row_width) * 64
        lanes = slice(tile * 128, tile * 128 + 128)
        top = part[pl.ds(pl.multiple_of(at, 32), 32), lanes]
        low = part[pl.ds(pl.multiple_of(at + 32, 32), 32), lanes]
        if lead:
            return jnp.where(lane_left, top, jnp.concatenate([low[:, 64:128], low[:, 0:64]], axis=1))
        return jnp.where(lane_left, jnp.concatenate([top[:, 64:128], top[:, 0:64]], axis=1), low)

    ranges = [(0, early), (early, row_width)]

    def rows_of(ref, h):
        lo, hi = ranges[h]
        return ref.at[pl.ds(lo, hi - lo)]

    def scopy(h):
        return pltpu.make_async_remote_copy(
            src_ref=rows_of(edge_sib.at[0], h), dst_ref=rows_of(edge_sib.at[1], h),
            send_sem=ssend_sem.at[h], recv_sem=srecv_sem.at[h],
            device_id=(row, sibling), device_id_type=MESH,
        )

    def ecopy(r, w, h):
        return pltpu.make_async_remote_copy(
            src_ref=rows_of(edge_out, h), dst_ref=rows_of(edge_in.at[row], h),
            send_sem=esend_sem.at[w, h], recv_sem=erecv_sem.at[row, h],
            device_id=(r, beside), device_id_type=MESH,
        )

    def ecome(r, h):
        return pltpu.make_async_remote_copy(
            src_ref=rows_of(edge_out, h), dst_ref=rows_of(edge_in.at[r], h),
            send_sem=esend_sem.at[0, h], recv_sem=erecv_sem.at[r, h],
            device_id=(r, beside), device_id_type=MESH,
        )

    def mcopy(source, w, target, h):
        return pltpu.make_async_remote_copy(
            src_ref=rows_of(mid_in.at[source], h), dst_ref=rows_of(mid_in.at[source], h),
            send_sem=msend_sem.at[w, h], recv_sem=mrecv_sem.at[source, h],
            device_id=(target, me), device_id_type=MESH,
        )

    def send_edges(h):
        for i in range(*ranges[h]):
            e0 = halves(i, 0, True).astype(jnp.bfloat16)
            e2 = halves(i, 1, True).astype(jnp.bfloat16)
            edge_sib[0, i] = jnp.where(first_core, e2, e0)
            edge_out[i] = jnp.where(first_core, e0, e2)
        scopy(h).start()

        @pl.when(has_beside)
        def _():
            for w, r in enumerate(other_row + [row]):
                ecopy(r, w, h).start()

    def send_mid(h):
        mids = [halves(i, 0, False) for i in range(*ranges[h])]
        scopy(h).wait_recv()
        for i, value in zip(range(*ranges[h]), mids):
            mid_in[row, i] = (value + edge_sib[1, i].astype(jnp.float32)).astype(jnp.bfloat16)
        for w, o in enumerate(other_row):
            mcopy(row, w, o, h).start()

    @pl.when(jnp.logical_not(has_beside))
    def _():
        edge_in[...] = jnp.zeros_like(edge_in)

    send_edges(0)
    send_mid(0)
    arrived([half_ring])
    dense(cooked + 2, cooked + 3)
    send_edges(1)
    send_mid(1)
    for h in range(2):
        @pl.when(has_beside)
        def _():
            for r in [row] + other_row:
                ecome(r, h).wait_recv()

        for o in other_row:
            mcopy(o, 0, o, h).wait_recv()
    panel_agg = n_col // n_row
    for a in range(n_col):
        pieces = []
        for r in range(n_row):
            at = a - r * panel_agg + 1
            if 0 <= at < row_width:
                here = lax.rem(at - first_row + 2 * row_width, row_width)
                there = lax.rem(at - first_beside + 2 * row_width, row_width)
                pieces.append(mid_in[r, here].astype(jnp.float32) + edge_in[r, there].astype(jnp.float32))
        full[a] = functools.reduce(jnp.add, pieces).astype(jnp.bfloat16)

    def dcopy(s):
        return pltpu.make_async_remote_copy(
            src_ref=outgoing.at[s], dst_ref=incoming.at[me], send_sem=send_sem.at[s], recv_sem=recv2_sem.at[me],
            device_id=(row, s), device_id_type=MESH,
        )

    def post(i, _):
        s = lax.rem(me + i, n_col)
        outgoing[s] = full[inverse[s]]
        dcopy(s).start()
        return 0

    lax.fori_loop(1, n_col, post, 0)
    incoming[me] = full[inverse[me]]

    for d in range(half_ring):
        for c in range(CHUNKS):
            if d < half_ring - 1 or c < half:
                go_right(shard_at(-d), c).wait_send()
                go_left(shard_at(d), (c + half) % CHUNKS).wait_send()
    for i in range(chips):
        go_over(i * CORES + k).wait_send()
    for w, o in enumerate(other_row):
        pcopy(w, o).wait_send()
        for h in range(2):
            mcopy(row, w, o, h).wait_send()
    for h in range(2):
        scopy(h).wait_send()

    @pl.when(has_beside)
    def _():
        for w, r in enumerate(other_row + [row]):
            for h in range(2):
                ecopy(r, w, h).wait_send()

    def arrive(i, _):
        c = lax.rem(me + n_col - i, n_col)
        pltpu.make_async_remote_copy(
            src_ref=outgoing.at[0], dst_ref=incoming.at[c], send_sem=send_sem.at[c], recv_sem=recv2_sem.at[c],
            device_id=(row, c), device_id_type=MESH,
        ).wait_recv()
        return 0

    lax.fori_loop(1, n_col, arrive, 0)

    def sent(i, _):
        dcopy(lax.rem(me + i, n_col)).wait_send()
        return 0

    lax.fori_loop(1, n_col, sent, 0)


def on_device(n_row, n_col, a_blocks, block_rows, block_cols, block_count, restrict, interp, aggregate, owner):
    vmem = pl.BlockSpec(memory_space=pltpu.VMEM)
    hbm = pl.BlockSpec(memory_space=pltpu.HBM)
    nb = restrict.shape[0]
    nj, piece = interp.shape[:2]
    slots = a_blocks.shape[2]
    agg_total = owner.shape[0]
    assert agg_total == n_col
    row_width = agg_total // n_row + 2
    bf16, f32, i32 = jnp.bfloat16, jnp.float32, jnp.int32
    chips = n_col // CORES
    panel = nb * n_col
    sized = jnp.transpose(a_blocks[0, 0], (1, 2, 0))
    dma = pltpu.SemaphoreType.DMA
    blocks = pl.pallas_call(
        functools.partial(coarse_kernel, n_row, n_col),
        out_shape=jax.ShapeDtypeStruct((n_col, 32, 128), bf16),
        in_specs=[hbm] * 8,
        out_specs=vmem,
        scratch_shapes=[
            pltpu.VMEM((1, slots), i32),
            pltpu.VMEM((1, slots), i32),
            pltpu.SMEM((1, 1), i32),
            pltpu.SMEM((aggregate.shape[0],), i32),
            pltpu.SMEM((agg_total,), i32),
            pltpu.VMEM((nb, 64, 64), bf16),
            pltpu.VMEM((nj, piece, 64), bf16),
            pltpu.VMEM((64, 64, slots), bf16),
            pltpu.VMEM((n_col, nb // 2, 64, 128), bf16),
            pltpu.VMEM((n_row, nj // 2, piece, 128), bf16),
            pltpu.VMEM((slots, 32, 128), f32),
            pltpu.VMEM((nj, 128, 128), bf16),
            pltpu.VMEM((slots + 1, 32, 128), bf16),
            pltpu.VMEM((slots + 1, 32, 128), bf16),
            pltpu.VMEM((slots, 128), i32),
            pltpu.VMEM((slots, 128), i32),
            pltpu.VMEM((1, slots), i32),
            pltpu.VMEM((1, panel * 4), i32),
            pltpu.SMEM((1, slots), i32),
            pltpu.SMEM((1, panel * 4), i32),
            pltpu.VMEM((panel // 2, 3, 16, 128), bf16),
            pltpu.VMEM((row_width * 64, 256), f32),
            pltpu.VMEM((row_width, 32, 128), bf16),
            pltpu.VMEM((2, row_width, 32, 128), bf16),
            pltpu.VMEM((n_row, row_width, 32, 128), bf16),
            pltpu.VMEM((n_row, row_width, 32, 128), bf16),
            pltpu.VMEM((n_col, 32, 128), bf16),
            pltpu.VMEM((n_col, 32, 128), bf16),
            pltpu.SMEM((n_col,), i32),
            dma((8,)),
            dma((2,)),
            dma((n_col, CHUNKS)),
            dma((n_col, CHUNKS)),
            dma((n_col,)),
            dma((n_col, CHUNKS)),
            dma((n_row,)),
            dma((n_row,)),
            dma((2,)),
            dma((2,)),
            dma((n_row, 2)),
            dma((n_row, 2)),
            dma((n_row, 2)),
            dma((n_row, 2)),
            dma((n_col,)),
            dma((n_col,)),
        ],
        compiler_params=pltpu.CompilerParams(collective_id=0, has_side_effects=True, vmem_limit_bytes=60 * 2**20),
        name="coarse_operator",
    )(block_rows[0], block_cols[0], block_count, aggregate, owner, restrict, interp, sized)
    return jnp.concatenate([blocks[:, :, :64], blocks[:, :, 64:]], axis=1).astype(f32)[None]


def solution(mesh):
    return jax.shard_map(
        functools.partial(on_device, mesh.shape["row"], mesh.shape["col"]),
        mesh=mesh,
        in_specs=(
            P("row", "col", None, None, None),
            P("row", "col", None),
            P("row", "col", None),
            P("row", "col"),
            P(("row", "col"), None, None),
            P("col", "row", None),
            P(),
            P(),
        ),
        out_specs=P("col", None, None, None),
        check_vma=False,
    )
```

```python
import functools

import jax
import jax.numpy as jnp
from jax import lax
from jax.experimental import pallas as pl
from jax.experimental.pallas import tpu as pltpu
from jax.sharding import PartitionSpec as P

MESH = pl.DeviceIdType.MESH
CORES = 2
DEPTH = 4
CHUNKS = 4
GROUP = 64
SLOT_BITS = 9
COL_BITS = 6
KEY_SHIFT = SLOT_BITS + COL_BITS


def coarse_kernel(
    n_row, n_col, rows_hbm, cols_hbm, count_hbm, agg_hbm, owner_hbm, r_hbm, p_hbm, a_hbm, incoming,
    rows_ref, cols_ref, count_ref, agg_ref, owner_ref, r_ref, p_ref, a_ref,
    rg_ref, pg_ref, flat, wide, sums, turned, v_col, rank_col, v_tab, last_tab, v_smem, last_smem, keep_ref, part,
    edge_out, edge_sib, edge_in, mid_in, full, outgoing, inverse,
    load_sem, tab_sem, right_sem, left_sem, sib_sem, recv_sem, psend_sem, precv_sem,
    ssend_sem, srecv_sem, esend_sem, erecv_sem, msend_sem, mrecv_sem, send_sem, recv2_sem,
):
    width = n_col // (CORES * DEPTH)
    chips = n_col // CORES
    half_ring = chips // 2
    me = lax.axis_index("col")
    row = lax.axis_index("row")
    z = me // (width * CORES)
    x = lax.rem(me // CORES, width)
    k = lax.rem(me, CORES)
    sibling = me + 1 - 2 * k
    beside = me - 1 + 2 * k
    has_beside = (beside >= 0) & (beside < n_col)
    other_row = [lax.rem(row + d, n_row) for d in range(1, n_row)]

    def spot_of(zz, xx):
        back = DEPTH - 1 - zz
        return jnp.where(
            xx == 0, zz, DEPTH + back * (width - 1) + jnp.where(lax.rem(back, 2) == 0, xx - 1, width - 1 - xx)
        )

    spot = spot_of(z, x)

    def chip_on(s):
        s = lax.rem(s + chips, chips)
        b = (s - DEPTH) // (width - 1)
        i = lax.rem(s - DEPTH, width - 1)
        far = (DEPTH - 1 - b) * width + jnp.where(lax.rem(b, 2) == 0, i + 1, width - 1 - i)
        return jnp.where(s < DEPTH, s * width, far)

    def chip_at(offset):
        return chip_on(spot + offset)

    def shard_at(offset):
        return chip_at(offset) * CORES + k

    right = shard_at(1)
    left = shard_at(-1)

    nb = r_ref.shape[0]
    tiles = nb // 2
    half_p = p_ref.shape[0] // 2
    piece = p_ref.shape[1]
    nj = p_ref.shape[0]
    slots = a_ref.shape[2]
    panel = nb * n_col
    per_agg = agg_ref.shape[0] // n_col
    row_width = part.shape[0] // 64

    loads = [
        pltpu.make_async_copy(src, dst, load_sem.at[i])
        for i, (src, dst) in enumerate(
            [
                (r_hbm, r_ref), (p_hbm, p_ref), (rows_hbm, rows_ref), (cols_hbm, cols_ref), (count_hbm, count_ref),
                (agg_hbm, agg_ref), (owner_hbm, owner_ref), (a_hbm, a_ref),
            ]
        )
    ]
    for load in loads:
        load.start()
    load_r, load_p, load_rows, load_cols, load_count, load_agg, load_owner, load_a = loads

    barrier = pltpu.get_barrier_semaphore()

    def greet(dev):
        pl.semaphore_signal(barrier, inc=1, device_id=dev, device_id_type=MESH)

    for near in (right, left, sibling):
        greet((row, near))
    for o in other_row:
        greet((o, me))

    @pl.when(has_beside)
    def _():
        for o in other_row:
            greet((o, beside))

    tile_ends = [(s, min(s + 128, slots)) for s in range(0, slots, 128)]

    table_copies = [
        pltpu.make_async_copy(v_tab, v_smem, tab_sem.at[0]), pltpu.make_async_copy(last_tab, last_smem, tab_sem.at[1])
    ]

    def tables():
        load_rows.wait()
        load_cols.wait()
        load_count.wait()
        load_agg.wait()
        cols = cols_ref[...]
        off = jnp.zeros_like(cols)
        for j in range(nj):
            off = jnp.where(cols == j, agg_ref[me * nj + j] - (me - 1), off)
        slot = lax.broadcasted_iota(jnp.int32, (1, slots), 1)
        key = jnp.where(slot < count_ref[0, 0], rows_ref[...] * 4 + off, panel * 4)
        v = (key * 2**COL_BITS + cols) * 2**SLOT_BITS + slot
        for s, e in tile_ends:
            v_col[s:e, :] = jnp.broadcast_to(v[:, s:e], (128, e - s)).T
        for s, e in tile_ends:
            below = (v_col[:, 0 : e - s] < v[:, s:e]).astype(jnp.int32)
            rank = jnp.sum(below, axis=0, keepdims=True)
            rank_col[s:e, :] = jnp.broadcast_to(rank, (128, e - s)).T
        for s, e in tile_ends:
            place = lax.broadcasted_iota(jnp.int32, (1, e - s), 1) + s
            hit = rank_col[:, 0 : e - s] == place
            v_tab[:, s:e] = jnp.sum(jnp.where(hit, v_col[:, 0 : e - s], 0), axis=0, keepdims=True)
        for s in range(0, panel * 4, 128):
            place = lax.broadcasted_iota(jnp.int32, (1, 128), 1) + s
            keys = v_col[...] >> KEY_SHIFT
            upto = jnp.sum((keys <= place).astype(jnp.int32), axis=0, keepdims=True)
            under = jnp.sum((keys < place).astype(jnp.int32), axis=0, keepdims=True)
            last_tab[:, s : s + 128] = jnp.where(upto > under, upto, 0)
        for c in table_copies:
            c.start()

    load_r.wait()
    for j in range(tiles):
        rg_ref[me, j] = jnp.concatenate([r_ref[2 * j], r_ref[2 * j + 1]], axis=1)
    pl.semaphore_wait(barrier, 3 + len(other_row) + jnp.where(has_beside, len(other_row), 0))

    size = tiles // CHUNKS
    half = CHUNKS // 2

    def ring(shard, c, sem, target):
        piece_of = rg_ref.at[shard, pl.ds(c * size, size)]
        return pltpu.make_async_remote_copy(
            src_ref=piece_of, dst_ref=piece_of, send_sem=sem.at[shard, c], recv_sem=recv_sem.at[shard, c],
            device_id=(row, target), device_id_type=MESH,
        )

    def go_right(shard, c):
        return ring(shard, c, right_sem, right)

    def go_left(shard, c):
        return ring(shard, c, left_sem, left)

    def go_over(shard):
        return pltpu.make_async_remote_copy(
            src_ref=rg_ref.at[shard], dst_ref=rg_ref.at[shard], send_sem=sib_sem.at[shard], recv_sem=recv_sem.at[shard, 0],
            device_id=(row, sibling), device_id_type=MESH,
        )

    def pcopy(way, target):
        return pltpu.make_async_remote_copy(
            src_ref=pg_ref.at[row], dst_ref=pg_ref.at[row], send_sem=psend_sem.at[way], recv_sem=precv_sem.at[row],
            device_id=(target, me), device_id_type=MESH,
        )

    for c in range(CHUNKS):
        go_right(me, c).start()
        go_left(me, (c + half) % CHUNKS).start()
    go_over(me).start()
    load_p.wait()
    for j in range(half_p):
        pg_ref[row, j, :, 0:64] = p_ref[j]
        pg_ref[row, j, :, 64:128] = p_ref[j + half_p]
    for w, o in enumerate(other_row):
        pcopy(w, o).start()

    def pass_on(d, c):
        back_c = (c + half) % CHUNKS
        onward = d < half_ring - 1 or c < half
        s = shard_at(-d)
        go_right(s, c).wait_recv()
        if onward:
            go_right(s, c).start()
        s = shard_at(d)
        go_left(s, back_c).wait_recv()
        if onward:
            go_left(s, back_c).start()
        if c == CHUNKS - 1:
            go_over(shard_at(-d)).start()
            go_over(shard_at(d)).start()

    def far_end():
        s = shard_at(half_ring)
        for c in range(CHUNKS):
            go_right(s, c).wait_recv()
        go_over(s).start()

    def turn():
        def body(g, _):
            for s, e in tile_ends:
                rows = []
                for t in range(16):
                    i = g * 16 + t
                    tall = jnp.concatenate([a_ref[i, :, s:e], a_ref[i + 32, :, s:e]], axis=0)
                    rows.append(tall.T.astype(jnp.float32))
                slotwise = jnp.transpose(jnp.stack(rows, axis=0), (1, 0, 2))
                flat[s:e, pl.ds(pl.multiple_of(g * 16, 16), 16), :] = slotwise.astype(jnp.bfloat16)
            return 0

        lax.fori_loop(0, 2, body, 0)

    def widen():
        for o in other_row:
            pltpu.make_async_remote_copy(
                src_ref=pg_ref.at[o], dst_ref=pg_ref.at[o], send_sem=psend_sem.at[0], recv_sem=precv_sem.at[o],
                device_id=(o, me), device_id_type=MESH,
            ).wait_recv()
        wide[...] = jnp.zeros_like(wide)

        def body(j, _):
            for r in range(n_row):
                lo, hi = r * piece, (r + 1) * piece
                both = pg_ref[r, j]
                wide[j, lo:hi, 0:64] = both[:, 0:64]
                wide[j, 64 + lo : 64 + hi, 64:128] = both[:, 0:64]
                wide[j + half_p, lo:hi, 0:64] = both[:, 64:128]
                wide[j + half_p, 64 + lo : 64 + hi, 64:128] = both[:, 64:128]
            return 0

        lax.fori_loop(0, half_p, body, 0, unroll=2)
        sums[0] = jnp.zeros((32, 128), jnp.bfloat16)
        turned[0] = jnp.zeros((32, 128), jnp.bfloat16)

    def multiply(lo, hi, run):
        def body(g, run):
            base = g * GROUP
            made = []
            for u in range(0, GROUP, 2):
                lefts, rights = [], []
                for w in range(2):
                    v = v_smem[0, base + u + w]
                    lefts.append(flat[v & (2**SLOT_BITS - 1)])
                    rights.append(wide[(v >> SLOT_BITS) & (2**COL_BITS - 1)])
                both = jnp.dot(
                    jnp.concatenate(lefts, axis=0), jnp.concatenate(rights, axis=1), preferred_element_type=jnp.float32
                ).astype(jnp.bfloat16)
                made += [both[0:32, 0:128], both[32:64, 128:256]]
            before = v_smem[0, jnp.maximum(base - 1, 0)] >> KEY_SHIFT
            for u in range(GROUP):
                now = v_smem[0, base + u] >> KEY_SHIFT
                run = run * jnp.where(now == before, 1.0, 0.0) + made[u].astype(jnp.float32)
                before = now
                both = run.astype(jnp.bfloat16)
                sums[base + u + 1] = both
                turned[base + u + 1] = jnp.concatenate([both[:, 64:128], both[:, 0:64]], axis=1)
            return run

        return lax.fori_loop(lo, hi, body, run)

    left_half = lax.broadcasted_iota(jnp.int32, (32, 128), 1) < 64
    left_row = lax.broadcasted_iota(jnp.int32, (16, 128), 1) < 64

    def masks():
        def body(s, _):
            floor = row * (n_col // n_row) + s * nb // per_agg - 1
            for j in range(tiles):
                first = row * panel + s * nb + 2 * j
                a0 = agg_ref[first] - floor
                a1 = agg_ref[first + 1] - floor
                for d in range(3):
                    keep = jnp.where(left_row, jnp.where(a0 == d, 1.0, 0.0), jnp.where(a1 == d, 1.0, 0.0))
                    keep_ref[s * tiles + j, d] = keep.astype(jnp.bfloat16)
            return 0

        lax.fori_loop(0, n_col, body, 0)

    def dense(lo, hi):
        def body(i, _):
            step = (i + 1) // 2
            chip = chip_at(jnp.where(lax.rem(i, 2) == 0, step, -step))
            base = chip * CORES * nb // per_agg
            total = None
            for t in range(CORES * tiles // 2):
                lefts = [[], [], []]
                rights = []
                for h in range(2):
                    s = chip * CORES + (2 * t + h) // tiles
                    j = (2 * t + h) % tiles
                    block = rg_ref[s, j]
                    for d in range(3):
                        lefts[d].append(block * jnp.concatenate([keep_ref[s * tiles + j, d]] * 4, axis=0))
                    for q in range(2):
                        at = (s * nb + 2 * j + q) * 4
                        i0, i1, i2 = (last_smem[0, at + ca] for ca in range(3))
                        upper = jnp.where(left_half, sums[i0], turned[i1])
                        lower = jnp.where(left_half, turned[i0], sums[i1])
                        rights.append(jnp.concatenate([upper, sums[i2]], axis=1))
                        rights.append(jnp.concatenate([lower, turned[i2]], axis=1))
                lhs = jnp.concatenate([jnp.concatenate(l, axis=1) for l in lefts], axis=0)
                rhs = jnp.concatenate(rights, axis=0)
                made = jnp.dot(lhs, rhs, preferred_element_type=jnp.float32)
                total = made if total is None else total + made
            at = pl.ds(pl.multiple_of(base * 64, 64), 192)
            part[at, :] = part[at, :] + total
            return 0

        lax.fori_loop(lo, hi, body, 0)

    def arrived(offsets):
        for o in offsets:
            go_over(chip_at(o) * CORES + 1 - k).wait_recv()

    def invert():
        load_owner.wait()

        def body(s, _):
            inverse[s] = lax.fori_loop(0, n_col, lambda t, got: jnp.where(owner_ref[t] == s, t, got), 0, unroll=True)
            return 0

        lax.fori_loop(0, n_col, body, 0)

    part[...] = jnp.zeros_like(part)
    load_a.wait()
    turn()
    run = jnp.zeros((32, 128), jnp.float32)
    groups = slots // GROUP
    done = 0
    cooked = 0
    pending = [0]
    for d in range(1, half_ring):
        for c in range(CHUNKS):
            pass_on(d, c)
            if c == CHUNKS - 1:
                pending += [-d, d]
            spot_no = (d - 1) * CHUNKS + c
            if spot_no == 0:
                tables()
            elif spot_no == 1:
                widen()
            elif spot_no == 2:
                masks()
                invert()
                for t in table_copies:
                    t.wait()
            elif done < groups:
                run = multiply(done, done + 1, run)
                done += 1
            elif len(pending) > 2 + 2 * (c == CHUNKS - 1):
                arrived(pending[:1])
                pending = pending[1:]
                dense(cooked, cooked + 1)
                cooked += 1
    if done < groups:
        run = multiply(done, groups, run)
    if pending[:-2]:
        arrived(pending[:-2])
        dense(cooked, cooked + len(pending) - 2)
        cooked += len(pending) - 2
    far_end()
    arrived(pending[-2:])
    dense(cooked, cooked + 2)

    lane_left = lax.broadcasted_iota(jnp.int32, (32, 128), 1) < 64
    first_core = k == 0
    early = row_width - 3

    def after_last(zz, xx):
        return chip_on(spot_of(zz, xx) + half_ring) * CORES * nb // per_agg + 3

    first_row = after_last(z, x)
    first_beside = after_last(beside // (width * CORES), lax.rem(beside // CORES, width))

    def halves(i, tile, lead):
        at = lax.rem(first_row + i, row_width) * 64
        lanes = slice(tile * 128, tile * 128 + 128)
        top = part[pl.ds(pl.multiple_of(at, 32), 32), lanes]
        low = part[pl.ds(pl.multiple_of(at + 32, 32), 32), lanes]
        if lead:
            return jnp.where(lane_left, top, jnp.concatenate([low[:, 64:128], low[:, 0:64]], axis=1))
        return jnp.where(lane_left, jnp.concatenate([top[:, 64:128], top[:, 0:64]], axis=1), low)

    ranges = [(0, early), (early, row_width)]

    def rows_of(ref, h):
        lo, hi = ranges[h]
        return ref.at[pl.ds(lo, hi - lo)]

    def scopy(h):
        return pltpu.make_async_remote_copy(
            src_ref=rows_of(edge_sib.at[0], h), dst_ref=rows_of(edge_sib.at[1], h),
            send_sem=ssend_sem.at[h], recv_sem=srecv_sem.at[h],
            device_id=(row, sibling), device_id_type=MESH,
        )

    def ecopy(r, w, h):
        return pltpu.make_async_remote_copy(
            src_ref=rows_of(edge_out, h), dst_ref=rows_of(edge_in.at[row], h),
            send_sem=esend_sem.at[w, h], recv_sem=erecv_sem.at[row, h],
            device_id=(r, beside), device_id_type=MESH,
        )

    def ecome(r, h):
        return pltpu.make_async_remote_copy(
            src_ref=rows_of(edge_out, h), dst_ref=rows_of(edge_in.at[r], h),
            send_sem=esend_sem.at[0, h], recv_sem=erecv_sem.at[r, h],
            device_id=(r, beside), device_id_type=MESH,
        )

    def mcopy(source, w, target, h):
        return pltpu.make_async_remote_copy(
            src_ref=rows_of(mid_in.at[source], h), dst_ref=rows_of(mid_in.at[source], h),
            send_sem=msend_sem.at[w, h], recv_sem=mrecv_sem.at[source, h],
            device_id=(target, me), device_id_type=MESH,
        )

    def send_edges(h):
        for i in range(*ranges[h]):
            e0 = halves(i, 0, True).astype(jnp.bfloat16)
            e2 = halves(i, 1, True).astype(jnp.bfloat16)
            edge_sib[0, i] = jnp.where(first_core, e2, e0)
            edge_out[i] = jnp.where(first_core, e0, e2)
        scopy(h).start()

        @pl.when(has_beside)
        def _():
            for w, r in enumerate(other_row + [row]):
                ecopy(r, w, h).start()

    def send_mid(h):
        mids = [halves(i, 0, False) for i in range(*ranges[h])]
        scopy(h).wait_recv()
        for i, value in zip(range(*ranges[h]), mids):
            mid_in[row, i] = (value + edge_sib[1, i].astype(jnp.float32)).astype(jnp.bfloat16)
        for w, o in enumerate(other_row):
            mcopy(row, w, o, h).start()

    @pl.when(jnp.logical_not(has_beside))
    def _():
        edge_in[...] = jnp.zeros_like(edge_in)

    send_edges(0)
    send_mid(0)
    arrived([half_ring])
    dense(cooked + 2, cooked + 3)
    send_edges(1)
    send_mid(1)
    for h in range(2):
        @pl.when(has_beside)
        def _():
            for r in [row] + other_row:
                ecome(r, h).wait_recv()

        for o in other_row:
            mcopy(o, 0, o, h).wait_recv()
    panel_agg = n_col // n_row
    for a in range(n_col):
        pieces = []
        for r in range(n_row):
            at = a - r * panel_agg + 1
            if 0 <= at < row_width:
                here = lax.rem(at - first_row + 2 * row_width, row_width)
                there = lax.rem(at - first_beside + 2 * row_width, row_width)
                pieces.append(mid_in[r, here].astype(jnp.float32) + edge_in[r, there].astype(jnp.float32))
        full[a] = functools.reduce(jnp.add, pieces).astype(jnp.bfloat16)

    def dcopy(s):
        return pltpu.make_async_remote_copy(
            src_ref=outgoing.at[s], dst_ref=incoming.at[me], send_sem=send_sem.at[s], recv_sem=recv2_sem.at[me],
            device_id=(row, s), device_id_type=MESH,
        )

    def post(i, _):
        s = jnp.where(z < DEPTH // 2, n_col - 1 - i, i)

        @pl.when(s != me)
        def _():
            outgoing[s] = full[inverse[s]]
            dcopy(s).start()

        return 0

    lax.fori_loop(0, n_col, post, 0)
    incoming[me] = full[inverse[me]]

    for d in range(half_ring):
        for c in range(CHUNKS):
            if d < half_ring - 1 or c < half:
                go_right(shard_at(-d), c).wait_send()
                go_left(shard_at(d), (c + half) % CHUNKS).wait_send()
    for i in range(chips):
        go_over(i * CORES + k).wait_send()
    for w, o in enumerate(other_row):
        pcopy(w, o).wait_send()
        for h in range(2):
            mcopy(row, w, o, h).wait_send()
    for h in range(2):
        scopy(h).wait_send()

    @pl.when(has_beside)
    def _():
        for w, r in enumerate(other_row + [row]):
            for h in range(2):
                ecopy(r, w, h).wait_send()

    def arrive(i, _):
        c = lax.rem(me + n_col - i, n_col)
        pltpu.make_async_remote_copy(
            src_ref=outgoing.at[0], dst_ref=incoming.at[c], send_sem=send_sem.at[c], recv_sem=recv2_sem.at[c],
            device_id=(row, c), device_id_type=MESH,
        ).wait_recv()
        return 0

    lax.fori_loop(1, n_col, arrive, 0)

    def sent(i, _):
        dcopy(lax.rem(me + i, n_col)).wait_send()
        return 0

    lax.fori_loop(1, n_col, sent, 0)


def unpack_kernel(blocks_ref, out_ref):
    for c in range(blocks_ref.shape[0]):
        block = blocks_ref[c].astype(jnp.float32)
        out_ref[0, c, 0:32, :] = block[:, 0:64]
        out_ref[0, c, 32:64, :] = block[:, 64:128]


def on_device(n_row, n_col, a_blocks, block_rows, block_cols, block_count, restrict, interp, aggregate, owner):
    vmem = pl.BlockSpec(memory_space=pltpu.VMEM)
    hbm = pl.BlockSpec(memory_space=pltpu.HBM)
    nb = restrict.shape[0]
    nj, piece = interp.shape[:2]
    slots = a_blocks.shape[2]
    agg_total = owner.shape[0]
    assert agg_total == n_col
    row_width = agg_total // n_row + 2
    bf16, f32, i32 = jnp.bfloat16, jnp.float32, jnp.int32
    chips = n_col // CORES
    panel = nb * n_col
    sized = jnp.transpose(a_blocks[0, 0], (1, 2, 0))
    dma = pltpu.SemaphoreType.DMA
    blocks = pl.pallas_call(
        functools.partial(coarse_kernel, n_row, n_col),
        out_shape=jax.ShapeDtypeStruct((n_col, 32, 128), bf16),
        in_specs=[hbm] * 8,
        out_specs=vmem,
        scratch_shapes=[
            pltpu.VMEM((1, slots), i32),
            pltpu.VMEM((1, slots), i32),
            pltpu.SMEM((1, 1), i32),
            pltpu.SMEM((aggregate.shape[0],), i32),
            pltpu.SMEM((agg_total,), i32),
            pltpu.VMEM((nb, 64, 64), bf16),
            pltpu.VMEM((nj, piece, 64), bf16),
            pltpu.VMEM((64, 64, slots), bf16),
            pltpu.VMEM((n_col, nb // 2, 64, 128), bf16),
            pltpu.VMEM((n_row, nj // 2, piece, 128), bf16),
            pltpu.VMEM((slots, 32, 128), bf16),
            pltpu.VMEM((nj, 128, 128), bf16),
            pltpu.VMEM((slots + 1, 32, 128), bf16),
            pltpu.VMEM((slots + 1, 32, 128), bf16),
            pltpu.VMEM((slots, 128), i32),
            pltpu.VMEM((slots, 128), i32),
            pltpu.VMEM((1, slots), i32),
            pltpu.VMEM((1, panel * 4), i32),
            pltpu.SMEM((1, slots), i32),
            pltpu.SMEM((1, panel * 4), i32),
            pltpu.VMEM((panel // 2, 3, 16, 128), bf16),
            pltpu.VMEM((row_width * 64, 256), f32),
            pltpu.VMEM((row_width, 32, 128), bf16),
            pltpu.VMEM((2, row_width, 32, 128), bf16),
            pltpu.VMEM((n_row, row_width, 32, 128), bf16),
            pltpu.VMEM((n_row, row_width, 32, 128), bf16),
            pltpu.VMEM((n_col, 32, 128), bf16),
            pltpu.VMEM((n_col, 32, 128), bf16),
            pltpu.SMEM((n_col,), i32),
            dma((8,)),
            dma((2,)),
            dma((n_col, CHUNKS)),
            dma((n_col, CHUNKS)),
            dma((n_col,)),
            dma((n_col, CHUNKS)),
            dma((n_row,)),
            dma((n_row,)),
            dma((2,)),
            dma((2,)),
            dma((n_row, 2)),
            dma((n_row, 2)),
            dma((n_row, 2)),
            dma((n_row, 2)),
            dma((n_col,)),
            dma((n_col,)),
        ],
        compiler_params=pltpu.CompilerParams(collective_id=0, has_side_effects=True, vmem_limit_bytes=55 * 2**20),
        name="coarse_operator",
    )(block_rows[0], block_cols[0], block_count, aggregate, owner, restrict, interp, sized)
    return pl.pallas_call(
        unpack_kernel,
        out_shape=jax.ShapeDtypeStruct((1, agg_total, 64, 64), f32),
        in_specs=[vmem],
        out_specs=vmem,
        name="unpack",
    )(blocks)


def solution(mesh):
    return jax.shard_map(
        functools.partial(on_device, mesh.shape["row"], mesh.shape["col"]),
        mesh=mesh,
        in_specs=(
            P("row", "col", None, None, None),
            P("row", "col", None),
            P("row", "col", None),
            P("row", "col"),
            P(("row", "col"), None, None),
            P("col", "row", None),
            P(),
            P(),
        ),
        out_specs=P("col", None, None, None),
        check_vma=False,
    )
```

```python
import functools

import jax
import jax.numpy as jnp
from jax import lax
from jax.experimental import pallas as pl
from jax.experimental.pallas import tpu as pltpu
from jax.sharding import PartitionSpec as P

MESH = pl.DeviceIdType.MESH
CORES = 2
DEPTH = 4
CHUNKS = 4
GROUP = 64
SLOT_BITS = 9
COL_BITS = 6
KEY_SHIFT = SLOT_BITS + COL_BITS


def coarse_kernel(
    n_row, n_col, rows_hbm, cols_hbm, count_hbm, agg_hbm, owner_hbm, r_hbm, p_hbm, a_hbm, incoming,
    rows_ref, cols_ref, count_ref, agg_ref, owner_ref, r_ref, p_ref, a_ref,
    rg_ref, pg_ref, flat, wide, sums, turned, v_col, rank_col, v_tab, last_tab, v_smem, last_smem, keep_ref, part,
    edge_out, edge_sib, edge_in, mid_in, full, outgoing, inverse,
    load_sem, tab_sem, right_sem, left_sem, sib_sem, recv_sem, psend_sem, precv_sem,
    ssend_sem, srecv_sem, esend_sem, erecv_sem, msend_sem, mrecv_sem, send_sem, recv2_sem,
):
    width = n_col // (CORES * DEPTH)
    chips = n_col // CORES
    half_ring = chips // 2
    me = lax.axis_index("col")
    row = lax.axis_index("row")
    z = me // (width * CORES)
    x = lax.rem(me // CORES, width)
    k = lax.rem(me, CORES)
    sibling = me + 1 - 2 * k
    beside = me - 1 + 2 * k
    has_beside = (beside >= 0) & (beside < n_col)
    other_row = [lax.rem(row + d, n_row) for d in range(1, n_row)]

    def spot_of(zz, xx):
        back = DEPTH - 1 - zz
        return jnp.where(
            xx == 0, zz, DEPTH + back * (width - 1) + jnp.where(lax.rem(back, 2) == 0, xx - 1, width - 1 - xx)
        )

    spot = spot_of(z, x)

    def chip_on(s):
        s = lax.rem(s + chips, chips)
        b = (s - DEPTH) // (width - 1)
        i = lax.rem(s - DEPTH, width - 1)
        far = (DEPTH - 1 - b) * width + jnp.where(lax.rem(b, 2) == 0, i + 1, width - 1 - i)
        return jnp.where(s < DEPTH, s * width, far)

    def chip_at(offset):
        return chip_on(spot + offset)

    def shard_at(offset):
        return chip_at(offset) * CORES + k

    right = shard_at(1)
    left = shard_at(-1)

    nb = r_ref.shape[0]
    tiles = nb // 2
    half_p = p_ref.shape[0] // 2
    piece = p_ref.shape[1]
    nj = p_ref.shape[0]
    slots = a_ref.shape[2]
    panel = nb * n_col
    per_agg = agg_ref.shape[0] // n_col
    row_width = part.shape[0] // 64

    barrier = pltpu.get_barrier_semaphore()

    def greet(dev):
        pl.semaphore_signal(barrier, inc=1, device_id=dev, device_id_type=MESH)

    for near in (right, left, sibling):
        greet((row, near))
    for o in other_row:
        greet((o, me))

    @pl.when(has_beside)
    def _():
        for o in other_row:
            greet((o, beside))

    loads = [
        pltpu.make_async_copy(src, dst, load_sem.at[i])
        for i, (src, dst) in enumerate(
            [
                (r_hbm, r_ref), (p_hbm, p_ref), (rows_hbm, rows_ref), (cols_hbm, cols_ref), (count_hbm, count_ref),
                (agg_hbm, agg_ref), (owner_hbm, owner_ref), (a_hbm, a_ref),
            ]
        )
    ]
    for load in loads:
        load.start()
    load_r, load_p, load_rows, load_cols, load_count, load_agg, load_owner, load_a = loads

    tile_ends = [(s, min(s + 128, slots)) for s in range(0, slots, 128)]

    table_copies = [
        pltpu.make_async_copy(v_tab, v_smem, tab_sem.at[0]), pltpu.make_async_copy(last_tab, last_smem, tab_sem.at[1])
    ]

    def tables():
        load_rows.wait()
        load_cols.wait()
        load_count.wait()
        cols = cols_ref[...]
        off = jnp.zeros_like(cols)
        for j in range(nj):
            off = jnp.where(cols == j, agg_ref[me * nj + j] - (me - 1), off)
        slot = lax.broadcasted_iota(jnp.int32, (1, slots), 1)
        key = jnp.where(slot < count_ref[0, 0], rows_ref[...] * 4 + off, panel * 4)
        v = (key * 2**COL_BITS + cols) * 2**SLOT_BITS + slot
        for s, e in tile_ends:
            v_col[s:e, :] = jnp.broadcast_to(v[:, s:e], (128, e - s)).T
        for s, e in tile_ends:
            below = (v_col[:, 0 : e - s] < v[:, s:e]).astype(jnp.int32)
            rank = jnp.sum(below, axis=0, keepdims=True)
            rank_col[s:e, :] = jnp.broadcast_to(rank, (128, e - s)).T
        for s, e in tile_ends:
            place = lax.broadcasted_iota(jnp.int32, (1, e - s), 1) + s
            hit = rank_col[:, 0 : e - s] == place
            v_tab[:, s:e] = jnp.sum(jnp.where(hit, v_col[:, 0 : e - s], 0), axis=0, keepdims=True)
        for s in range(0, panel * 4, 128):
            place = lax.broadcasted_iota(jnp.int32, (1, 128), 1) + s
            keys = v_col[...] >> KEY_SHIFT
            upto = jnp.sum((keys <= place).astype(jnp.int32), axis=0, keepdims=True)
            under = jnp.sum((keys < place).astype(jnp.int32), axis=0, keepdims=True)
            last_tab[:, s : s + 128] = jnp.where(upto > under, upto, 0)
        for c in table_copies:
            c.start()

    load_r.wait()
    for j in range(tiles):
        rg_ref[me, j] = jnp.concatenate([r_ref[2 * j], r_ref[2 * j + 1]], axis=1)
    pl.semaphore_wait(barrier, 3 + len(other_row) + jnp.where(has_beside, len(other_row), 0))

    size = tiles // CHUNKS
    half = CHUNKS // 2

    def ring(shard, c, sem, target):
        piece_of = rg_ref.at[shard, pl.ds(c * size, size)]
        return pltpu.make_async_remote_copy(
            src_ref=piece_of, dst_ref=piece_of, send_sem=sem.at[shard, c], recv_sem=recv_sem.at[shard, c],
            device_id=(row, target), device_id_type=MESH,
        )

    def go_right(shard, c):
        return ring(shard, c, right_sem, right)

    def go_left(shard, c):
        return ring(shard, c, left_sem, left)

    def go_over(shard):
        return pltpu.make_async_remote_copy(
            src_ref=rg_ref.at[shard], dst_ref=rg_ref.at[shard], send_sem=sib_sem.at[shard], recv_sem=recv_sem.at[shard, 0],
            device_id=(row, sibling), device_id_type=MESH,
        )

    def pcopy(way, target):
        return pltpu.make_async_remote_copy(
            src_ref=pg_ref.at[row], dst_ref=pg_ref.at[row], send_sem=psend_sem.at[way], recv_sem=precv_sem.at[row],
            device_id=(target, me), device_id_type=MESH,
        )

    for c in range(CHUNKS):
        go_right(me, c).start()
        go_left(me, (c + half) % CHUNKS).start()
    go_over(me).start()
    load_p.wait()
    for j in range(half_p):
        pg_ref[row, j, :, 0:64] = p_ref[j]
        pg_ref[row, j, :, 64:128] = p_ref[j + half_p]
    for w, o in enumerate(other_row):
        pcopy(w, o).start()

    def pass_on(d, c):
        back_c = (c + half) % CHUNKS
        onward = d < half_ring - 1 or c < half
        s = shard_at(-d)
        go_right(s, c).wait_recv()
        if onward:
            go_right(s, c).start()
        s = shard_at(d)
        go_left(s, back_c).wait_recv()
        if onward:
            go_left(s, back_c).start()
        if c == CHUNKS - 1:
            go_over(shard_at(-d)).start()
            go_over(shard_at(d)).start()

    def far_end():
        s = shard_at(half_ring)
        for c in range(CHUNKS):
            go_right(s, c).wait_recv()
        go_over(s).start()

    def turn():
        def body(g, _):
            for s, e in tile_ends:
                rows = []
                for t in range(16):
                    i = g * 16 + t
                    tall = jnp.concatenate([a_ref[i, :, s:e], a_ref[i + 32, :, s:e]], axis=0)
                    rows.append(tall.T.astype(jnp.float32))
                slotwise = jnp.transpose(jnp.stack(rows, axis=0), (1, 0, 2))
                flat[s:e, pl.ds(pl.multiple_of(g * 16, 16), 16), :] = slotwise.astype(jnp.bfloat16)
            return 0

        lax.fori_loop(0, 2, body, 0)

    def widen():
        for o in other_row:
            pltpu.make_async_remote_copy(
                src_ref=pg_ref.at[o], dst_ref=pg_ref.at[o], send_sem=psend_sem.at[0], recv_sem=precv_sem.at[o],
                device_id=(o, me), device_id_type=MESH,
            ).wait_recv()
        wide[...] = jnp.zeros_like(wide)

        def body(j, _):
            for r in range(n_row):
                lo, hi = r * piece, (r + 1) * piece
                both = pg_ref[r, j]
                wide[j, lo:hi, 0:64] = both[:, 0:64]
                wide[j, 64 + lo : 64 + hi, 64:128] = both[:, 0:64]
                wide[j + half_p, lo:hi, 0:64] = both[:, 64:128]
                wide[j + half_p, 64 + lo : 64 + hi, 64:128] = both[:, 64:128]
            return 0

        lax.fori_loop(0, half_p, body, 0, unroll=2)
        sums[0] = jnp.zeros((32, 128), jnp.bfloat16)
        turned[0] = jnp.zeros((32, 128), jnp.bfloat16)

    def multiply(lo, hi, run):
        def body(g, run):
            base = g * GROUP
            made = []
            for u in range(0, GROUP, 2):
                lefts, rights = [], []
                for w in range(2):
                    v = v_smem[0, base + u + w]
                    lefts.append(flat[v & (2**SLOT_BITS - 1)])
                    rights.append(wide[(v >> SLOT_BITS) & (2**COL_BITS - 1)])
                both = jnp.dot(
                    jnp.concatenate(lefts, axis=0), jnp.concatenate(rights, axis=1), preferred_element_type=jnp.float32
                ).astype(jnp.bfloat16)
                made += [both[0:32, 0:128], both[32:64, 128:256]]
            before = v_smem[0, jnp.maximum(base - 1, 0)] >> KEY_SHIFT
            for u in range(GROUP):
                now = v_smem[0, base + u] >> KEY_SHIFT
                run = run * jnp.where(now == before, 1.0, 0.0) + made[u].astype(jnp.float32)
                before = now
                both = run.astype(jnp.bfloat16)
                sums[base + u + 1] = both
                turned[base + u + 1] = jnp.concatenate([both[:, 64:128], both[:, 0:64]], axis=1)
            return run

        return lax.fori_loop(lo, hi, body, run)

    left_half = lax.broadcasted_iota(jnp.int32, (32, 128), 1) < 64
    left_row = lax.broadcasted_iota(jnp.int32, (16, 128), 1) < 64

    def masks():
        load_agg.wait()
        def body(s, _):
            floor = row * (n_col // n_row) + s * nb // per_agg - 1
            for j in range(tiles):
                first = row * panel + s * nb + 2 * j
                a0 = agg_ref[first] - floor
                a1 = agg_ref[first + 1] - floor
                for d in range(3):
                    keep = jnp.where(left_row, jnp.where(a0 == d, 1.0, 0.0), jnp.where(a1 == d, 1.0, 0.0))
                    keep_ref[s * tiles + j, d] = keep.astype(jnp.bfloat16)
            return 0

        lax.fori_loop(0, n_col, body, 0)

    def dense(lo, hi):
        def body(i, _):
            step = (i + 1) // 2
            chip = chip_at(jnp.where(lax.rem(i, 2) == 0, step, -step))
            base = chip * CORES * nb // per_agg
            total = None
            for t in range(CORES * tiles // 2):
                lefts = [[], [], []]
                rights = []
                for h in range(2):
                    s = chip * CORES + (2 * t + h) // tiles
                    j = (2 * t + h) % tiles
                    block = rg_ref[s, j]
                    for d in range(3):
                        lefts[d].append(block * jnp.concatenate([keep_ref[s * tiles + j, d]] * 4, axis=0))
                    for q in range(2):
                        at = (s * nb + 2 * j + q) * 4
                        i0, i1, i2 = (last_smem[0, at + ca] for ca in range(3))
                        upper = jnp.where(left_half, sums[i0], turned[i1])
                        lower = jnp.where(left_half, turned[i0], sums[i1])
                        rights.append(jnp.concatenate([upper, sums[i2]], axis=1))
                        rights.append(jnp.concatenate([lower, turned[i2]], axis=1))
                lhs = jnp.concatenate([jnp.concatenate(l, axis=1) for l in lefts], axis=0)
                rhs = jnp.concatenate(rights, axis=0)
                made = jnp.dot(lhs, rhs, preferred_element_type=jnp.float32)
                total = made if total is None else total + made
            at = pl.ds(pl.multiple_of(base * 64, 64), 192)
            part[at, :] = part[at, :] + total
            return 0

        lax.fori_loop(lo, hi, body, 0)

    def arrived(offsets):
        for o in offsets:
            go_over(chip_at(o) * CORES + 1 - k).wait_recv()

    def invert():
        load_owner.wait()

        def body(s, _):
            inverse[s] = lax.fori_loop(0, n_col, lambda t, got: jnp.where(owner_ref[t] == s, t, got), 0, unroll=True)
            return 0

        lax.fori_loop(0, n_col, body, 0)

    part[...] = jnp.zeros_like(part)
    load_a.wait()
    turn()
    run = jnp.zeros((32, 128), jnp.float32)
    groups = slots // GROUP
    done = 0
    cooked = 0
    pending = [0]
    for d in range(1, half_ring):
        for c in range(CHUNKS):
            pass_on(d, c)
            if c == CHUNKS - 1:
                pending += [-d, d]
            spot_no = (d - 1) * CHUNKS + c
            if spot_no == 0:
                masks()
            elif spot_no == 1:
                invert()
            elif spot_no == 2:
                tables()
            elif spot_no == 3:
                widen()
                for t in table_copies:
                    t.wait()
            elif done < groups:
                run = multiply(done, done + 1, run)
                done += 1
            elif len(pending) > 2 + 2 * (c == CHUNKS - 1):
                arrived(pending[:1])
                pending = pending[1:]
                dense(cooked, cooked + 1)
                cooked += 1
    if done < groups:
        run = multiply(done, groups, run)
    if pending[:-2]:
        arrived(pending[:-2])
        dense(cooked, cooked + len(pending) - 2)
        cooked += len(pending) - 2
    far_end()
    arrived(pending[-2:])
    dense(cooked, cooked + 2)

    lane_left = lax.broadcasted_iota(jnp.int32, (32, 128), 1) < 64
    first_core = k == 0
    early = row_width - 3

    def after_last(zz, xx):
        return chip_on(spot_of(zz, xx) + half_ring) * CORES * nb // per_agg + 3

    first_row = after_last(z, x)
    first_beside = after_last(beside // (width * CORES), lax.rem(beside // CORES, width))

    def halves(i, tile, lead):
        at = lax.rem(first_row + i, row_width) * 64
        lanes = slice(tile * 128, tile * 128 + 128)
        top = part[pl.ds(pl.multiple_of(at, 32), 32), lanes]
        low = part[pl.ds(pl.multiple_of(at + 32, 32), 32), lanes]
        if lead:
            return jnp.where(lane_left, top, jnp.concatenate([low[:, 64:128], low[:, 0:64]], axis=1))
        return jnp.where(lane_left, jnp.concatenate([top[:, 64:128], top[:, 0:64]], axis=1), low)

    ranges = [(0, early), (early, row_width)]

    def rows_of(ref, h):
        lo, hi = ranges[h]
        return ref.at[pl.ds(lo, hi - lo)]

    def scopy(h):
        return pltpu.make_async_remote_copy(
            src_ref=rows_of(edge_sib.at[0], h), dst_ref=rows_of(edge_sib.at[1], h),
            send_sem=ssend_sem.at[h], recv_sem=srecv_sem.at[h],
            device_id=(row, sibling), device_id_type=MESH,
        )

    def ecopy(r, w, h):
        return pltpu.make_async_remote_copy(
            src_ref=rows_of(edge_out, h), dst_ref=rows_of(edge_in.at[row], h),
            send_sem=esend_sem.at[w, h], recv_sem=erecv_sem.at[row, h],
            device_id=(r, beside), device_id_type=MESH,
        )

    def ecome(r, h):
        return pltpu.make_async_remote_copy(
            src_ref=rows_of(edge_out, h), dst_ref=rows_of(edge_in.at[r], h),
            send_sem=esend_sem.at[0, h], recv_sem=erecv_sem.at[r, h],
            device_id=(r, beside), device_id_type=MESH,
        )

    def mcopy(source, w, target, h):
        return pltpu.make_async_remote_copy(
            src_ref=rows_of(mid_in.at[source], h), dst_ref=rows_of(mid_in.at[source], h),
            send_sem=msend_sem.at[w, h], recv_sem=mrecv_sem.at[source, h],
            device_id=(target, me), device_id_type=MESH,
        )

    def send_edges(h):
        for i in range(*ranges[h]):
            e0 = halves(i, 0, True).astype(jnp.bfloat16)
            e2 = halves(i, 1, True).astype(jnp.bfloat16)
            edge_sib[0, i] = jnp.where(first_core, e2, e0)
            edge_out[i] = jnp.where(first_core, e0, e2)
        scopy(h).start()

        @pl.when(has_beside)
        def _():
            for w, r in enumerate(other_row + [row]):
                ecopy(r, w, h).start()

    def send_mid(h):
        mids = [halves(i, 0, False) for i in range(*ranges[h])]
        scopy(h).wait_recv()
        for i, value in zip(range(*ranges[h]), mids):
            mid_in[row, i] = (value + edge_sib[1, i].astype(jnp.float32)).astype(jnp.bfloat16)
        for w, o in enumerate(other_row):
            mcopy(row, w, o, h).start()

    @pl.when(jnp.logical_not(has_beside))
    def _():
        edge_in[...] = jnp.zeros_like(edge_in)

    send_edges(0)
    send_mid(0)
    arrived([half_ring])
    dense(cooked + 2, cooked + 3)
    send_edges(1)
    send_mid(1)
    for h in range(2):
        @pl.when(has_beside)
        def _():
            for r in [row] + other_row:
                ecome(r, h).wait_recv()

        for o in other_row:
            mcopy(o, 0, o, h).wait_recv()
    panel_agg = n_col // n_row
    for a in range(n_col):
        pieces = []
        for r in range(n_row):
            at = a - r * panel_agg + 1
            if 0 <= at < row_width:
                here = lax.rem(at - first_row + 2 * row_width, row_width)
                there = lax.rem(at - first_beside + 2 * row_width, row_width)
                pieces.append(mid_in[r, here].astype(jnp.float32) + edge_in[r, there].astype(jnp.float32))
        full[a] = functools.reduce(jnp.add, pieces).astype(jnp.bfloat16)

    def dcopy(s):
        return pltpu.make_async_remote_copy(
            src_ref=outgoing.at[s], dst_ref=incoming.at[me], send_sem=send_sem.at[s], recv_sem=recv2_sem.at[me],
            device_id=(row, s), device_id_type=MESH,
        )

    def post(i, _):
        s = jnp.where(z < DEPTH // 2, n_col - 1 - i, i)

        @pl.when(s != me)
        def _():
            outgoing[s] = full[inverse[s]]
            dcopy(s).start()

        return 0

    lax.fori_loop(0, n_col, post, 0)
    incoming[me] = full[inverse[me]]

    for d in range(half_ring):
        for c in range(CHUNKS):
            if d < half_ring - 1 or c < half:
                go_right(shard_at(-d), c).wait_send()
                go_left(shard_at(d), (c + half) % CHUNKS).wait_send()
    for i in range(chips):
        go_over(i * CORES + k).wait_send()
    for w, o in enumerate(other_row):
        pcopy(w, o).wait_send()
        for h in range(2):
            mcopy(row, w, o, h).wait_send()
    for h in range(2):
        scopy(h).wait_send()

    @pl.when(has_beside)
    def _():
        for w, r in enumerate(other_row + [row]):
            for h in range(2):
                ecopy(r, w, h).wait_send()

    def arrive(i, _):
        c = lax.rem(me + n_col - i, n_col)
        pltpu.make_async_remote_copy(
            src_ref=outgoing.at[0], dst_ref=incoming.at[c], send_sem=send_sem.at[c], recv_sem=recv2_sem.at[c],
            device_id=(row, c), device_id_type=MESH,
        ).wait_recv()
        return 0

    lax.fori_loop(1, n_col, arrive, 0)

    def sent(i, _):
        dcopy(lax.rem(me + i, n_col)).wait_send()
        return 0

    lax.fori_loop(1, n_col, sent, 0)


def unpack_kernel(blocks_ref, out_ref):
    for c in range(blocks_ref.shape[0]):
        block = blocks_ref[c].astype(jnp.float32)
        out_ref[0, c, 0:32, :] = block[:, 0:64]
        out_ref[0, c, 32:64, :] = block[:, 64:128]


def on_device(n_row, n_col, a_blocks, block_rows, block_cols, block_count, restrict, interp, aggregate, owner):
    vmem = pl.BlockSpec(memory_space=pltpu.VMEM)
    hbm = pl.BlockSpec(memory_space=pltpu.HBM)
    nb = restrict.shape[0]
    nj, piece = interp.shape[:2]
    slots = a_blocks.shape[2]
    agg_total = owner.shape[0]
    assert agg_total == n_col
    row_width = agg_total // n_row + 2
    bf16, f32, i32 = jnp.bfloat16, jnp.float32, jnp.int32
    chips = n_col // CORES
    panel = nb * n_col
    sized = jnp.transpose(a_blocks[0, 0], (1, 2, 0))
    dma = pltpu.SemaphoreType.DMA
    blocks = pl.pallas_call(
        functools.partial(coarse_kernel, n_row, n_col),
        out_shape=jax.ShapeDtypeStruct((n_col, 32, 128), bf16),
        in_specs=[hbm] * 8,
        out_specs=vmem,
        scratch_shapes=[
            pltpu.VMEM((1, slots), i32),
            pltpu.VMEM((1, slots), i32),
            pltpu.SMEM((1, 1), i32),
            pltpu.SMEM((aggregate.shape[0],), i32),
            pltpu.SMEM((agg_total,), i32),
            pltpu.VMEM((nb, 64, 64), bf16),
            pltpu.VMEM((nj, piece, 64), bf16),
            pltpu.VMEM((64, 64, slots), bf16),
            pltpu.VMEM((n_col, nb // 2, 64, 128), bf16),
            pltpu.VMEM((n_row, nj // 2, piece, 128), bf16),
            pltpu.VMEM((slots, 32, 128), bf16),
            pltpu.VMEM((nj, 128, 128), bf16),
            pltpu.VMEM((slots + 1, 32, 128), bf16),
            pltpu.VMEM((slots + 1, 32, 128), bf16),
            pltpu.VMEM((slots, 128), i32),
            pltpu.VMEM((slots, 128), i32),
            pltpu.VMEM((1, slots), i32),
            pltpu.VMEM((1, panel * 4), i32),
            pltpu.SMEM((1, slots), i32),
            pltpu.SMEM((1, panel * 4), i32),
            pltpu.VMEM((panel // 2, 3, 16, 128), bf16),
            pltpu.VMEM((row_width * 64, 256), f32),
            pltpu.VMEM((row_width, 32, 128), bf16),
            pltpu.VMEM((2, row_width, 32, 128), bf16),
            pltpu.VMEM((n_row, row_width, 32, 128), bf16),
            pltpu.VMEM((n_row, row_width, 32, 128), bf16),
            pltpu.VMEM((n_col, 32, 128), bf16),
            pltpu.VMEM((n_col, 32, 128), bf16),
            pltpu.SMEM((n_col,), i32),
            dma((8,)),
            dma((2,)),
            dma((n_col, CHUNKS)),
            dma((n_col, CHUNKS)),
            dma((n_col,)),
            dma((n_col, CHUNKS)),
            dma((n_row,)),
            dma((n_row,)),
            dma((2,)),
            dma((2,)),
            dma((n_row, 2)),
            dma((n_row, 2)),
            dma((n_row, 2)),
            dma((n_row, 2)),
            dma((n_col,)),
            dma((n_col,)),
        ],
        compiler_params=pltpu.CompilerParams(collective_id=0, has_side_effects=True, vmem_limit_bytes=55 * 2**20),
        name="coarse_operator",
    )(block_rows[0], block_cols[0], block_count, aggregate, owner, restrict, interp, sized)
    return pl.pallas_call(
        unpack_kernel,
        out_shape=jax.ShapeDtypeStruct((1, agg_total, 64, 64), f32),
        in_specs=[vmem],
        out_specs=vmem,
        name="unpack",
    )(blocks)


def solution(mesh):
    return jax.shard_map(
        functools.partial(on_device, mesh.shape["row"], mesh.shape["col"]),
        mesh=mesh,
        in_specs=(
            P("row", "col", None, None, None),
            P("row", "col", None),
            P("row", "col", None),
            P("row", "col"),
            P(("row", "col"), None, None),
            P("col", "row", None),
            P(),
            P(),
        ),
        out_specs=P("col", None, None, None),
        check_vma=False,
    )
```

```python
import functools

import jax
import jax.numpy as jnp
from jax import lax
from jax.experimental import pallas as pl
from jax.experimental.pallas import tpu as pltpu
from jax.sharding import PartitionSpec as P

MESH = pl.DeviceIdType.MESH
CORES = 2
DEPTH = 4
CHUNKS = 4
GROUP = 64
SLOT_BITS = 9
COL_BITS = 6
KEY_SHIFT = SLOT_BITS + COL_BITS


def coarse_kernel(
    n_row, n_col, rows_hbm, cols_hbm, count_hbm, agg_hbm, owner_hbm, r_hbm, p_hbm, a_hbm, incoming,
    rows_ref, cols_ref, count_ref, agg_ref, owner_ref, r_ref, p_ref, a_ref,
    rg_ref, pg_ref, flat, wide, sums, turned, v_col, rank_col, v_tab, last_tab, v_smem, last_smem, keep_ref, part,
    edge_out, edge_sib, edge_in, mid_in, full, outgoing, inverse,
    load_sem, tab_sem, right_sem, left_sem, sib_sem, recv_sem, psend_sem, precv_sem,
    ssend_sem, srecv_sem, esend_sem, erecv_sem, msend_sem, mrecv_sem, send_sem, recv2_sem,
):
    width = n_col // (CORES * DEPTH)
    chips = n_col // CORES
    half_ring = chips // 2
    me = lax.axis_index("col")
    row = lax.axis_index("row")
    z = me // (width * CORES)
    x = lax.rem(me // CORES, width)
    k = lax.rem(me, CORES)
    sibling = me + 1 - 2 * k
    beside = me - 1 + 2 * k
    has_beside = (beside >= 0) & (beside < n_col)
    other_row = [lax.rem(row + d, n_row) for d in range(1, n_row)]

    def spot_of(zz, xx):
        back = DEPTH - 1 - zz
        return jnp.where(
            xx == 0, zz, DEPTH + back * (width - 1) + jnp.where(lax.rem(back, 2) == 0, xx - 1, width - 1 - xx)
        )

    spot = spot_of(z, x)

    def chip_on(s):
        s = lax.rem(s + chips, chips)
        b = (s - DEPTH) // (width - 1)
        i = lax.rem(s - DEPTH, width - 1)
        far = (DEPTH - 1 - b) * width + jnp.where(lax.rem(b, 2) == 0, i + 1, width - 1 - i)
        return jnp.where(s < DEPTH, s * width, far)

    def chip_at(offset):
        return chip_on(spot + offset)

    def shard_at(offset):
        return chip_at(offset) * CORES + k

    right = shard_at(1)
    left = shard_at(-1)

    nb = r_ref.shape[0]
    tiles = nb // 2
    half_p = p_ref.shape[0] // 2
    piece = p_ref.shape[1]
    nj = p_ref.shape[0]
    slots = a_ref.shape[2]
    panel = nb * n_col
    per_agg = agg_ref.shape[0] // n_col
    row_width = part.shape[0] // 64

    barrier = pltpu.get_barrier_semaphore()

    def greet(dev):
        pl.semaphore_signal(barrier, inc=1, device_id=dev, device_id_type=MESH)

    for near in (right, left, sibling):
        greet((row, near))
    for o in other_row:
        greet((o, me))

    @pl.when(has_beside)
    def _():
        for o in other_row:
            greet((o, beside))

    loads = [
        pltpu.make_async_copy(src, dst, load_sem.at[i])
        for i, (src, dst) in enumerate(
            [
                (r_hbm, r_ref), (p_hbm, p_ref), (rows_hbm, rows_ref), (cols_hbm, cols_ref), (count_hbm, count_ref),
                (agg_hbm, agg_ref), (owner_hbm, owner_ref), (a_hbm, a_ref),
            ]
        )
    ]
    for load in loads:
        load.start()
    load_r, load_p, load_rows, load_cols, load_count, load_agg, load_owner, load_a = loads

    tile_ends = [(s, min(s + 128, slots)) for s in range(0, slots, 128)]

    table_copies = [
        pltpu.make_async_copy(v_tab, v_smem, tab_sem.at[0]), pltpu.make_async_copy(last_tab, last_smem, tab_sem.at[1])
    ]

    def tables():
        load_rows.wait()
        load_cols.wait()
        load_count.wait()
        cols = cols_ref[...]
        off = jnp.zeros_like(cols)
        for j in range(nj):
            off = jnp.where(cols == j, agg_ref[me * nj + j] - (me - 1), off)
        slot = lax.broadcasted_iota(jnp.int32, (1, slots), 1)
        key = jnp.where(slot < count_ref[0, 0], rows_ref[...] * 4 + off, panel * 4)
        v = (key * 2**COL_BITS + cols) * 2**SLOT_BITS + slot
        for s, e in tile_ends:
            v_col[s:e, :] = jnp.broadcast_to(v[:, s:e], (128, e - s)).T
        for s, e in tile_ends:
            below = (v_col[:, 0 : e - s] < v[:, s:e]).astype(jnp.int32)
            rank = jnp.sum(below, axis=0, keepdims=True)
            rank_col[s:e, :] = jnp.broadcast_to(rank, (128, e - s)).T
        for s, e in tile_ends:
            place = lax.broadcasted_iota(jnp.int32, (1, e - s), 1) + s
            hit = rank_col[:, 0 : e - s] == place
            v_tab[:, s:e] = jnp.sum(jnp.where(hit, v_col[:, 0 : e - s], 0), axis=0, keepdims=True)
        for s in range(0, panel * 4, 128):
            place = lax.broadcasted_iota(jnp.int32, (1, 128), 1) + s
            keys = v_col[...] >> KEY_SHIFT
            upto = jnp.sum((keys <= place).astype(jnp.int32), axis=0, keepdims=True)
            under = jnp.sum((keys < place).astype(jnp.int32), axis=0, keepdims=True)
            last_tab[:, s : s + 128] = jnp.where(upto > under, upto, 0)
        for c in table_copies:
            c.start()

    load_r.wait()
    for j in range(tiles):
        rg_ref[me, j] = jnp.concatenate([r_ref[2 * j], r_ref[2 * j + 1]], axis=1)
    pl.semaphore_wait(barrier, 3 + len(other_row) + jnp.where(has_beside, len(other_row), 0))

    size = tiles // CHUNKS
    half = CHUNKS // 2

    def ring(shard, c, sem, target):
        piece_of = rg_ref.at[shard, pl.ds(c * size, size)]
        return pltpu.make_async_remote_copy(
            src_ref=piece_of, dst_ref=piece_of, send_sem=sem.at[shard, c], recv_sem=recv_sem.at[shard, c],
            device_id=(row, target), device_id_type=MESH,
        )

    def go_right(shard, c):
        return ring(shard, c, right_sem, right)

    def go_left(shard, c):
        return ring(shard, c, left_sem, left)

    def go_over(shard):
        return pltpu.make_async_remote_copy(
            src_ref=rg_ref.at[shard], dst_ref=rg_ref.at[shard], send_sem=sib_sem.at[shard], recv_sem=recv_sem.at[shard, 0],
            device_id=(row, sibling), device_id_type=MESH,
        )

    def pcopy(way, target):
        return pltpu.make_async_remote_copy(
            src_ref=pg_ref.at[row], dst_ref=pg_ref.at[row], send_sem=psend_sem.at[way], recv_sem=precv_sem.at[row],
            device_id=(target, me), device_id_type=MESH,
        )

    for c in range(CHUNKS):
        go_right(me, c).start()
        go_left(me, (c + half) % CHUNKS).start()
    go_over(me).start()
    load_p.wait()
    for j in range(half_p):
        pg_ref[row, j, :, 0:64] = p_ref[j]
        pg_ref[row, j, :, 64:128] = p_ref[j + half_p]
    for w, o in enumerate(other_row):
        pcopy(w, o).start()

    def pass_on(d, c):
        back_c = (c + half) % CHUNKS
        onward = d < half_ring - 1 or c < half
        s = shard_at(-d)
        go_right(s, c).wait_recv()
        if onward:
            go_right(s, c).start()
        if c == CHUNKS - 1:
            go_over(s).start()
        s = shard_at(d)
        go_left(s, back_c).wait_recv()
        if onward:
            go_left(s, back_c).start()
        if c == CHUNKS - 1:
            go_over(s).start()

    def far_end():
        s = shard_at(half_ring)
        for c in range(CHUNKS):
            go_right(s, c).wait_recv()
        go_over(s).start()

    def turn():
        def body(g, _):
            for s, e in tile_ends:
                rows = []
                for t in range(16):
                    i = g * 16 + t
                    tall = jnp.concatenate([a_ref[i, :, s:e], a_ref[i + 32, :, s:e]], axis=0)
                    rows.append(tall.T.astype(jnp.float32))
                slotwise = jnp.transpose(jnp.stack(rows, axis=0), (1, 0, 2))
                flat[s:e, pl.ds(pl.multiple_of(g * 16, 16), 16), :] = slotwise.astype(jnp.bfloat16)
            return 0

        lax.fori_loop(0, 2, body, 0)

    def widen():
        for o in other_row:
            pltpu.make_async_remote_copy(
                src_ref=pg_ref.at[o], dst_ref=pg_ref.at[o], send_sem=psend_sem.at[0], recv_sem=precv_sem.at[o],
                device_id=(o, me), device_id_type=MESH,
            ).wait_recv()
        wide[...] = jnp.zeros_like(wide)

        def body(j, _):
            for r in range(n_row):
                lo, hi = r * piece, (r + 1) * piece
                both = pg_ref[r, j]
                wide[j, lo:hi, 0:64] = both[:, 0:64]
                wide[j, 64 + lo : 64 + hi, 64:128] = both[:, 0:64]
                wide[j + half_p, lo:hi, 0:64] = both[:, 64:128]
                wide[j + half_p, 64 + lo : 64 + hi, 64:128] = both[:, 64:128]
            return 0

        lax.fori_loop(0, half_p, body, 0, unroll=2)
        sums[0] = jnp.zeros((32, 128), jnp.bfloat16)
        turned[0] = jnp.zeros((32, 128), jnp.bfloat16)

    def multiply(lo, hi, run):
        def body(g, run):
            base = g * GROUP
            made = []
            for u in range(0, GROUP, 2):
                lefts, rights = [], []
                for w in range(2):
                    v = v_smem[0, base + u + w]
                    lefts.append(flat[v & (2**SLOT_BITS - 1)])
                    rights.append(wide[(v >> SLOT_BITS) & (2**COL_BITS - 1)])
                both = jnp.dot(
                    jnp.concatenate(lefts, axis=0), jnp.concatenate(rights, axis=1), preferred_element_type=jnp.float32
                ).astype(jnp.bfloat16)
                made += [both[0:32, 0:128], both[32:64, 128:256]]
            before = v_smem[0, jnp.maximum(base - 1, 0)] >> KEY_SHIFT
            for u in range(GROUP):
                now = v_smem[0, base + u] >> KEY_SHIFT
                run = run * jnp.where(now == before, 1.0, 0.0) + made[u].astype(jnp.float32)
                before = now
                both = run.astype(jnp.bfloat16)
                sums[base + u + 1] = both
                turned[base + u + 1] = jnp.concatenate([both[:, 64:128], both[:, 0:64]], axis=1)
            return run

        return lax.fori_loop(lo, hi, body, run)

    left_half = lax.broadcasted_iota(jnp.int32, (32, 128), 1) < 64
    left_row = lax.broadcasted_iota(jnp.int32, (16, 128), 1) < 64

    def masks():
        load_agg.wait()
        def body(s, _):
            floor = row * (n_col // n_row) + s * nb // per_agg - 1
            for j in range(tiles):
                first = row * panel + s * nb + 2 * j
                a0 = agg_ref[first] - floor
                a1 = agg_ref[first + 1] - floor
                for d in range(3):
                    keep = jnp.where(left_row, jnp.where(a0 == d, 1.0, 0.0), jnp.where(a1 == d, 1.0, 0.0))
                    keep_ref[s * tiles + j, d] = keep.astype(jnp.bfloat16)
            return 0

        lax.fori_loop(0, n_col, body, 0)

    def dense(lo, hi):
        def body(i, _):
            step = (i + 1) // 2
            chip = chip_at(jnp.where(lax.rem(i, 2) == 0, step, -step))
            base = chip * CORES * nb // per_agg
            total = None
            for t in range(CORES * tiles // 2):
                lefts = [[], [], []]
                rights = []
                for h in range(2):
                    s = chip * CORES + (2 * t + h) // tiles
                    j = (2 * t + h) % tiles
                    block = rg_ref[s, j]
                    for d in range(3):
                        lefts[d].append(block * jnp.concatenate([keep_ref[s * tiles + j, d]] * 4, axis=0))
                    for q in range(2):
                        at = (s * nb + 2 * j + q) * 4
                        i0, i1, i2 = (last_smem[0, at + ca] for ca in range(3))
                        upper = jnp.where(left_half, sums[i0], turned[i1])
                        lower = jnp.where(left_half, turned[i0], sums[i1])
                        rights.append(jnp.concatenate([upper, sums[i2]], axis=1))
                        rights.append(jnp.concatenate([lower, turned[i2]], axis=1))
                lhs = jnp.concatenate([jnp.concatenate(l, axis=1) for l in lefts], axis=0)
                rhs = jnp.concatenate(rights, axis=0)
                made = jnp.dot(lhs, rhs, preferred_element_type=jnp.float32)
                total = made if total is None else total + made
            at = pl.ds(pl.multiple_of(base * 64, 64), 192)
            part[at, :] = part[at, :] + total
            return 0

        lax.fori_loop(lo, hi, body, 0)

    def arrived(offsets):
        for o in offsets:
            go_over(chip_at(o) * CORES + 1 - k).wait_recv()

    def invert():
        load_owner.wait()

        def body(s, _):
            inverse[s] = lax.fori_loop(0, n_col, lambda t, got: jnp.where(owner_ref[t] == s, t, got), 0, unroll=True)
            return 0

        lax.fori_loop(0, n_col, body, 0)

    part[...] = jnp.zeros_like(part)
    load_a.wait()
    turn()
    run = jnp.zeros((32, 128), jnp.float32)
    groups = slots // GROUP
    done = 0
    cooked = 0
    pending = [0]
    for d in range(1, half_ring):
        for c in range(CHUNKS):
            pass_on(d, c)
            if c == CHUNKS - 1:
                pending += [-d, d]
            spot_no = (d - 1) * CHUNKS + c
            if spot_no == 0:
                masks()
            elif spot_no == 1:
                invert()
            elif spot_no == 2:
                tables()
            elif spot_no == 3:
                widen()
                for t in table_copies:
                    t.wait()
            elif done < groups:
                run = multiply(done, done + 1, run)
                done += 1
            elif len(pending) > 2 + 2 * (c == CHUNKS - 1):
                arrived(pending[:1])
                pending = pending[1:]
                dense(cooked, cooked + 1)
                cooked += 1
    if done < groups:
        run = multiply(done, groups, run)
    if pending[:-2]:
        arrived(pending[:-2])
        dense(cooked, cooked + len(pending) - 2)
        cooked += len(pending) - 2
    far_end()
    arrived(pending[-2:])
    dense(cooked, cooked + 2)

    lane_left = lax.broadcasted_iota(jnp.int32, (32, 128), 1) < 64
    first_core = k == 0
    early = row_width - 3

    def after_last(zz, xx):
        return chip_on(spot_of(zz, xx) + half_ring) * CORES * nb // per_agg + 3

    first_row = after_last(z, x)
    first_beside = after_last(beside // (width * CORES), lax.rem(beside // CORES, width))

    def halves(i, tile, lead):
        at = lax.rem(first_row + i, row_width) * 64
        lanes = slice(tile * 128, tile * 128 + 128)
        top = part[pl.ds(pl.multiple_of(at, 32), 32), lanes]
        low = part[pl.ds(pl.multiple_of(at + 32, 32), 32), lanes]
        if lead:
            return jnp.where(lane_left, top, jnp.concatenate([low[:, 64:128], low[:, 0:64]], axis=1))
        return jnp.where(lane_left, jnp.concatenate([top[:, 64:128], top[:, 0:64]], axis=1), low)

    ranges = [(0, early), (early, row_width)]

    def rows_of(ref, h):
        lo, hi = ranges[h]
        return ref.at[pl.ds(lo, hi - lo)]

    def scopy(h):
        return pltpu.make_async_remote_copy(
            src_ref=rows_of(edge_sib.at[0], h), dst_ref=rows_of(edge_sib.at[1], h),
            send_sem=ssend_sem.at[h], recv_sem=srecv_sem.at[h],
            device_id=(row, sibling), device_id_type=MESH,
        )

    def ecopy(r, w, h):
        return pltpu.make_async_remote_copy(
            src_ref=rows_of(edge_out, h), dst_ref=rows_of(edge_in.at[row], h),
            send_sem=esend_sem.at[w, h], recv_sem=erecv_sem.at[row, h],
            device_id=(r, beside), device_id_type=MESH,
        )

    def ecome(r, h):
        return pltpu.make_async_remote_copy(
            src_ref=rows_of(edge_out, h), dst_ref=rows_of(edge_in.at[r], h),
            send_sem=esend_sem.at[0, h], recv_sem=erecv_sem.at[r, h],
            device_id=(r, beside), device_id_type=MESH,
        )

    def mcopy(source, w, target, h):
        return pltpu.make_async_remote_copy(
            src_ref=rows_of(mid_in.at[source], h), dst_ref=rows_of(mid_in.at[source], h),
            send_sem=msend_sem.at[w, h], recv_sem=mrecv_sem.at[source, h],
            device_id=(target, me), device_id_type=MESH,
        )

    def send_edges(h):
        for i in range(*ranges[h]):
            e0 = halves(i, 0, True).astype(jnp.bfloat16)
            e2 = halves(i, 1, True).astype(jnp.bfloat16)
            edge_sib[0, i] = jnp.where(first_core, e2, e0)
            edge_out[i] = jnp.where(first_core, e0, e2)
        scopy(h).start()

        @pl.when(has_beside)
        def _():
            for w, r in enumerate(other_row + [row]):
                ecopy(r, w, h).start()

    def send_mid(h):
        mids = [halves(i, 0, False) for i in range(*ranges[h])]
        scopy(h).wait_recv()
        for i, value in zip(range(*ranges[h]), mids):
            mid_in[row, i] = (value + edge_sib[1, i].astype(jnp.float32)).astype(jnp.bfloat16)
        for w, o in enumerate(other_row):
            mcopy(row, w, o, h).start()

    @pl.when(jnp.logical_not(has_beside))
    def _():
        edge_in[...] = jnp.zeros_like(edge_in)

    send_edges(0)
    send_mid(0)
    arrived([half_ring])
    dense(cooked + 2, cooked + 3)
    send_edges(1)
    send_mid(1)
    for h in range(2):
        @pl.when(has_beside)
        def _():
            for r in [row] + other_row:
                ecome(r, h).wait_recv()

        for o in other_row:
            mcopy(o, 0, o, h).wait_recv()
    panel_agg = n_col // n_row
    for a in range(n_col):
        pieces = []
        for r in range(n_row):
            at = a - r * panel_agg + 1
            if 0 <= at < row_width:
                here = lax.rem(at - first_row + 2 * row_width, row_width)
                there = lax.rem(at - first_beside + 2 * row_width, row_width)
                pieces.append(mid_in[r, here].astype(jnp.float32) + edge_in[r, there].astype(jnp.float32))
        full[a] = functools.reduce(jnp.add, pieces).astype(jnp.bfloat16)

    def dcopy(s):
        return pltpu.make_async_remote_copy(
            src_ref=outgoing.at[s], dst_ref=incoming.at[me], send_sem=send_sem.at[s], recv_sem=recv2_sem.at[me],
            device_id=(row, s), device_id_type=MESH,
        )

    def post(i, _):
        s = jnp.where(z < DEPTH // 2, n_col - 1 - i, i)

        @pl.when(s != me)
        def _():
            outgoing[s] = full[inverse[s]]
            dcopy(s).start()

        return 0

    lax.fori_loop(0, n_col, post, 0, unroll=4)
    incoming[me] = full[inverse[me]]

    for d in range(half_ring):
        for c in range(CHUNKS):
            if d < half_ring - 1 or c < half:
                go_right(shard_at(-d), c).wait_send()
                go_left(shard_at(d), (c + half) % CHUNKS).wait_send()
    for i in range(chips):
        go_over(i * CORES + k).wait_send()
    for w, o in enumerate(other_row):
        pcopy(w, o).wait_send()
        for h in range(2):
            mcopy(row, w, o, h).wait_send()
    for h in range(2):
        scopy(h).wait_send()

    @pl.when(has_beside)
    def _():
        for w, r in enumerate(other_row + [row]):
            for h in range(2):
                ecopy(r, w, h).wait_send()

    def arrive(i, _):
        c = lax.rem(me + n_col - i, n_col)
        pltpu.make_async_remote_copy(
            src_ref=outgoing.at[0], dst_ref=incoming.at[c], send_sem=send_sem.at[c], recv_sem=recv2_sem.at[c],
            device_id=(row, c), device_id_type=MESH,
        ).wait_recv()
        return 0

    lax.fori_loop(1, n_col, arrive, 0)

    def sent(i, _):
        dcopy(lax.rem(me + i, n_col)).wait_send()
        return 0

    lax.fori_loop(1, n_col, sent, 0)


def unpack_kernel(blocks_ref, out_ref):
    for c in range(blocks_ref.shape[0]):
        block = blocks_ref[c].astype(jnp.float32)
        out_ref[0, c, 0:32, :] = block[:, 0:64]
        out_ref[0, c, 32:64, :] = block[:, 64:128]


def on_device(n_row, n_col, a_blocks, block_rows, block_cols, block_count, restrict, interp, aggregate, owner):
    vmem = pl.BlockSpec(memory_space=pltpu.VMEM)
    hbm = pl.BlockSpec(memory_space=pltpu.HBM)
    nb = restrict.shape[0]
    nj, piece = interp.shape[:2]
    slots = a_blocks.shape[2]
    agg_total = owner.shape[0]
    assert agg_total == n_col
    row_width = agg_total // n_row + 2
    bf16, f32, i32 = jnp.bfloat16, jnp.float32, jnp.int32
    chips = n_col // CORES
    panel = nb * n_col
    sized = jnp.transpose(a_blocks[0, 0], (1, 2, 0))
    dma = pltpu.SemaphoreType.DMA
    blocks = pl.pallas_call(
        functools.partial(coarse_kernel, n_row, n_col),
        out_shape=jax.ShapeDtypeStruct((n_col, 32, 128), bf16),
        in_specs=[hbm] * 8,
        out_specs=vmem,
        scratch_shapes=[
            pltpu.VMEM((1, slots), i32),
            pltpu.VMEM((1, slots), i32),
            pltpu.SMEM((1, 1), i32),
            pltpu.SMEM((aggregate.shape[0],), i32),
            pltpu.SMEM((agg_total,), i32),
            pltpu.VMEM((nb, 64, 64), bf16),
            pltpu.VMEM((nj, piece, 64), bf16),
            pltpu.VMEM((64, 64, slots), bf16),
            pltpu.VMEM((n_col, nb // 2, 64, 128), bf16),
            pltpu.VMEM((n_row, nj // 2, piece, 128), bf16),
            pltpu.VMEM((slots, 32, 128), bf16),
            pltpu.VMEM((nj, 128, 128), bf16),
            pltpu.VMEM((slots + 1, 32, 128), bf16),
            pltpu.VMEM((slots + 1, 32, 128), bf16),
            pltpu.VMEM((slots, 128), i32),
            pltpu.VMEM((slots, 128), i32),
            pltpu.VMEM((1, slots), i32),
            pltpu.VMEM((1, panel * 4), i32),
            pltpu.SMEM((1, slots), i32),
            pltpu.SMEM((1, panel * 4), i32),
            pltpu.VMEM((panel // 2, 3, 16, 128), bf16),
            pltpu.VMEM((row_width * 64, 256), f32),
            pltpu.VMEM((row_width, 32, 128), bf16),
            pltpu.VMEM((2, row_width, 32, 128), bf16),
            pltpu.VMEM((n_row, row_width, 32, 128), bf16),
            pltpu.VMEM((n_row, row_width, 32, 128), bf16),
            pltpu.VMEM((n_col, 32, 128), bf16),
            pltpu.VMEM((n_col, 32, 128), bf16),
            pltpu.SMEM((n_col,), i32),
            dma((8,)),
            dma((2,)),
            dma((n_col, CHUNKS)),
            dma((n_col, CHUNKS)),
            dma((n_col,)),
            dma((n_col, CHUNKS)),
            dma((n_row,)),
            dma((n_row,)),
            dma((2,)),
            dma((2,)),
            dma((n_row, 2)),
            dma((n_row, 2)),
            dma((n_row, 2)),
            dma((n_row, 2)),
            dma((n_col,)),
            dma((n_col,)),
        ],
        compiler_params=pltpu.CompilerParams(collective_id=0, has_side_effects=True, vmem_limit_bytes=55 * 2**20),
        name="coarse_operator",
    )(block_rows[0], block_cols[0], block_count, aggregate, owner, restrict, interp, sized)
    return pl.pallas_call(
        unpack_kernel,
        out_shape=jax.ShapeDtypeStruct((1, agg_total, 64, 64), f32),
        in_specs=[vmem],
        out_specs=vmem,
        name="unpack",
    )(blocks)


def solution(mesh):
    return jax.shard_map(
        functools.partial(on_device, mesh.shape["row"], mesh.shape["col"]),
        mesh=mesh,
        in_specs=(
            P("row", "col", None, None, None),
            P("row", "col", None),
            P("row", "col", None),
            P("row", "col"),
            P(("row", "col"), None, None),
            P("col", "row", None),
            P(),
            P(),
        ),
        out_specs=P("col", None, None, None),
        check_vma=False,
    )
```

```python
import functools

import jax
import jax.numpy as jnp
from jax import lax
from jax.experimental import pallas as pl
from jax.experimental.pallas import tpu as pltpu
from jax.sharding import PartitionSpec as P

MESH = pl.DeviceIdType.MESH
CORES = 2
DEPTH = 4
CHUNKS = 4
GROUP = 64
SLOT_BITS = 9
COL_BITS = 6
KEY_SHIFT = SLOT_BITS + COL_BITS


def coarse_kernel(
    n_row, n_col, rows_hbm, cols_hbm, count_hbm, agg_hbm, owner_hbm, r_hbm, p_hbm, a_hbm, incoming,
    rows_ref, cols_ref, count_ref, agg_ref, owner_ref, r_ref, p_ref, a_ref,
    rg_ref, pg_ref, flat, wide, sums, turned, v_col, rank_col, v_tab, last_tab, v_smem, last_smem, keep_ref, part,
    edge_out, edge_sib, edge_in, mid_in, full, outgoing, inverse,
    load_sem, tab_sem, right_sem, left_sem, sib_sem, recv_sem, psend_sem, precv_sem,
    ssend_sem, srecv_sem, esend_sem, erecv_sem, msend_sem, mrecv_sem, send_sem, recv2_sem,
):
    width = n_col // (CORES * DEPTH)
    chips = n_col // CORES
    half_ring = chips // 2
    me = lax.axis_index("col")
    row = lax.axis_index("row")
    z = me // (width * CORES)
    x = lax.rem(me // CORES, width)
    k = lax.rem(me, CORES)
    sibling = me + 1 - 2 * k
    beside = me - 1 + 2 * k
    has_beside = (beside >= 0) & (beside < n_col)
    other_row = [lax.rem(row + d, n_row) for d in range(1, n_row)]

    def spot_of(zz, xx):
        back = DEPTH - 1 - zz
        return jnp.where(
            xx == 0, zz, DEPTH + back * (width - 1) + jnp.where(lax.rem(back, 2) == 0, xx - 1, width - 1 - xx)
        )

    spot = spot_of(z, x)

    def chip_on(s):
        s = lax.rem(s + chips, chips)
        b = (s - DEPTH) // (width - 1)
        i = lax.rem(s - DEPTH, width - 1)
        far = (DEPTH - 1 - b) * width + jnp.where(lax.rem(b, 2) == 0, i + 1, width - 1 - i)
        return jnp.where(s < DEPTH, s * width, far)

    def chip_at(offset):
        return chip_on(spot + offset)

    def shard_at(offset):
        return chip_at(offset) * CORES + k

    right = shard_at(1)
    left = shard_at(-1)

    nb = r_ref.shape[0]
    tiles = nb // 2
    half_p = p_ref.shape[0] // 2
    piece = p_ref.shape[1]
    nj = p_ref.shape[0]
    slots = a_ref.shape[2]
    panel = nb * n_col
    per_agg = agg_ref.shape[0] // n_col
    row_width = part.shape[0] // 64

    barrier = pltpu.get_barrier_semaphore()

    def greet(dev):
        pl.semaphore_signal(barrier, inc=1, device_id=dev, device_id_type=MESH)

    for near in (right, left, sibling):
        greet((row, near))
    for o in other_row:
        greet((o, me))

    @pl.when(has_beside)
    def _():
        for o in other_row:
            greet((o, beside))

    loads = [
        pltpu.make_async_copy(src, dst, load_sem.at[i])
        for i, (src, dst) in enumerate(
            [
                (r_hbm, r_ref), (p_hbm, p_ref), (rows_hbm, rows_ref), (cols_hbm, cols_ref), (count_hbm, count_ref),
                (agg_hbm, agg_ref), (owner_hbm, owner_ref), (a_hbm, a_ref),
            ]
        )
    ]
    for load in loads:
        load.start()
    load_r, load_p, load_rows, load_cols, load_count, load_agg, load_owner, load_a = loads

    tile_ends = [(s, min(s + 128, slots)) for s in range(0, slots, 128)]

    table_copies = [
        pltpu.make_async_copy(v_tab, v_smem, tab_sem.at[0]), pltpu.make_async_copy(last_tab, last_smem, tab_sem.at[1])
    ]

    def tables():
        load_rows.wait()
        load_cols.wait()
        load_count.wait()
        cols = cols_ref[...]
        off = jnp.zeros_like(cols)
        for j in range(nj):
            off = jnp.where(cols == j, agg_ref[me * nj + j] - (me - 1), off)
        slot = lax.broadcasted_iota(jnp.int32, (1, slots), 1)
        key = jnp.where(slot < count_ref[0, 0], rows_ref[...] * 4 + off, panel * 4)
        v = (key * 2**COL_BITS + cols) * 2**SLOT_BITS + slot
        for s, e in tile_ends:
            v_col[s:e, :] = jnp.broadcast_to(v[:, s:e], (128, e - s)).T
        for s, e in tile_ends:
            below = (v_col[:, 0 : e - s] < v[:, s:e]).astype(jnp.int32)
            rank = jnp.sum(below, axis=0, keepdims=True)
            rank_col[s:e, :] = jnp.broadcast_to(rank, (128, e - s)).T
        for s, e in tile_ends:
            place = lax.broadcasted_iota(jnp.int32, (1, e - s), 1) + s
            hit = rank_col[:, 0 : e - s] == place
            v_tab[:, s:e] = jnp.sum(jnp.where(hit, v_col[:, 0 : e - s], 0), axis=0, keepdims=True)
        for s in range(0, panel * 4, 128):
            place = lax.broadcasted_iota(jnp.int32, (1, 128), 1) + s
            keys = v_col[...] >> KEY_SHIFT
            upto = jnp.sum((keys <= place).astype(jnp.int32), axis=0, keepdims=True)
            under = jnp.sum((keys < place).astype(jnp.int32), axis=0, keepdims=True)
            last_tab[:, s : s + 128] = jnp.where(upto > under, upto, 0)
        for c in table_copies:
            c.start()

    load_r.wait()
    for j in range(tiles):
        rg_ref[me, j] = jnp.concatenate([r_ref[2 * j], r_ref[2 * j + 1]], axis=1)
    pl.semaphore_wait(barrier, 3 + len(other_row) + jnp.where(has_beside, len(other_row), 0))

    size = tiles // CHUNKS
    half = CHUNKS // 2

    def ring(shard, c, sem, target):
        piece_of = rg_ref.at[shard, pl.ds(c * size, size)]
        return pltpu.make_async_remote_copy(
            src_ref=piece_of, dst_ref=piece_of, send_sem=sem.at[shard, c], recv_sem=recv_sem.at[shard, c],
            device_id=(row, target), device_id_type=MESH,
        )

    def go_right(shard, c):
        return ring(shard, c, right_sem, right)

    def go_left(shard, c):
        return ring(shard, c, left_sem, left)

    def go_over(shard):
        return pltpu.make_async_remote_copy(
            src_ref=rg_ref.at[shard], dst_ref=rg_ref.at[shard], send_sem=sib_sem.at[shard], recv_sem=recv_sem.at[shard, 0],
            device_id=(row, sibling), device_id_type=MESH,
        )

    def pcopy(way, target):
        return pltpu.make_async_remote_copy(
            src_ref=pg_ref.at[row], dst_ref=pg_ref.at[row], send_sem=psend_sem.at[way], recv_sem=precv_sem.at[row],
            device_id=(target, me), device_id_type=MESH,
        )

    for c in range(CHUNKS):
        go_right(me, c).start()
        go_left(me, (c + half) % CHUNKS).start()
    go_over(me).start()
    load_p.wait()
    for j in range(half_p):
        pg_ref[row, j, :, 0:64] = p_ref[j]
        pg_ref[row, j, :, 64:128] = p_ref[j + half_p]
    for w, o in enumerate(other_row):
        pcopy(w, o).start()

    def pass_on(d, c):
        back_c = (c + half) % CHUNKS
        onward = d < half_ring - 1 or c < half
        s = shard_at(-d)
        go_right(s, c).wait_recv()
        if onward:
            go_right(s, c).start()
        s = shard_at(d)
        go_left(s, back_c).wait_recv()
        if onward:
            go_left(s, back_c).start()
        if c == CHUNKS - 1:
            go_over(shard_at(-d)).start()
            go_over(shard_at(d)).start()

    def far_end():
        s = shard_at(half_ring)
        for c in range(CHUNKS):
            go_right(s, c).wait_recv()
        go_over(s).start()

    def turn():
        def body(g, _):
            for s, e in tile_ends:
                rows = []
                for t in range(16):
                    i = g * 16 + t
                    tall = jnp.concatenate([a_ref[i, :, s:e], a_ref[i + 32, :, s:e]], axis=0)
                    rows.append(tall.T.astype(jnp.float32))
                slotwise = jnp.transpose(jnp.stack(rows, axis=0), (1, 0, 2))
                flat[s:e, pl.ds(pl.multiple_of(g * 16, 16), 16), :] = slotwise.astype(jnp.bfloat16)
            return 0

        lax.fori_loop(0, 2, body, 0)

    def widen():
        for o in other_row:
            pltpu.make_async_remote_copy(
                src_ref=pg_ref.at[o], dst_ref=pg_ref.at[o], send_sem=psend_sem.at[0], recv_sem=precv_sem.at[o],
                device_id=(o, me), device_id_type=MESH,
            ).wait_recv()

        def body(j, _):
            for r in range(n_row):
                lo, hi = r * piece, (r + 1) * piece
                both = pg_ref[r, j]
                wide[j, lo:hi, 0:64] = both[:, 0:64]
                wide[j, 64 + lo : 64 + hi, 64:128] = both[:, 0:64]
                wide[j + half_p, lo:hi, 0:64] = both[:, 64:128]
                wide[j + half_p, 64 + lo : 64 + hi, 64:128] = both[:, 64:128]
            return 0

        lax.fori_loop(0, half_p, body, 0, unroll=2)
        sums[0] = jnp.zeros((32, 128), jnp.bfloat16)
        turned[0] = jnp.zeros((32, 128), jnp.bfloat16)

    def multiply(lo, hi, run):
        def body(g, run):
            base = g * GROUP
            made = []
            for u in range(0, GROUP, 2):
                lefts, rights = [], []
                for w in range(2):
                    v = v_smem[0, base + u + w]
                    lefts.append(flat[v & (2**SLOT_BITS - 1)])
                    rights.append(wide[(v >> SLOT_BITS) & (2**COL_BITS - 1)])
                both = jnp.dot(
                    jnp.concatenate(lefts, axis=0), jnp.concatenate(rights, axis=1), preferred_element_type=jnp.float32
                ).astype(jnp.bfloat16)
                made += [both[0:32, 0:128], both[32:64, 128:256]]
            before = v_smem[0, jnp.maximum(base - 1, 0)] >> KEY_SHIFT
            for u in range(GROUP):
                now = v_smem[0, base + u] >> KEY_SHIFT
                run = run * jnp.where(now == before, 1.0, 0.0) + made[u].astype(jnp.float32)
                before = now
                both = run.astype(jnp.bfloat16)
                sums[base + u + 1] = both
                turned[base + u + 1] = jnp.concatenate([both[:, 64:128], both[:, 0:64]], axis=1)
            return run

        return lax.fori_loop(lo, hi, body, run)

    left_half = lax.broadcasted_iota(jnp.int32, (32, 128), 1) < 64
    left_row = lax.broadcasted_iota(jnp.int32, (16, 128), 1) < 64

    def masks():
        load_agg.wait()
        def body(s, _):
            floor = row * (n_col // n_row) + s * nb // per_agg - 1
            for j in range(tiles):
                first = row * panel + s * nb + 2 * j
                a0 = agg_ref[first] - floor
                a1 = agg_ref[first + 1] - floor
                for d in range(3):
                    keep = jnp.where(left_row, jnp.where(a0 == d, 1.0, 0.0), jnp.where(a1 == d, 1.0, 0.0))
                    keep_ref[s * tiles + j, d] = keep.astype(jnp.bfloat16)
            return 0

        lax.fori_loop(0, n_col, body, 0)

    def dense(lo, hi):
        def body(i, _):
            step = (i + 1) // 2
            chip = chip_at(jnp.where(lax.rem(i, 2) == 0, step, -step))
            base = chip * CORES * nb // per_agg
            total = None
            for t in range(CORES * tiles // 2):
                lefts = [[], [], []]
                rights = []
                for h in range(2):
                    s = chip * CORES + (2 * t + h) // tiles
                    j = (2 * t + h) % tiles
                    block = rg_ref[s, j]
                    for d in range(3):
                        lefts[d].append(block * jnp.concatenate([keep_ref[s * tiles + j, d]] * 4, axis=0))
                    for q in range(2):
                        at = (s * nb + 2 * j + q) * 4
                        i0, i1, i2 = (last_smem[0, at + ca] for ca in range(3))
                        upper = jnp.where(left_half, sums[i0], turned[i1])
                        lower = jnp.where(left_half, turned[i0], sums[i1])
                        rights.append(jnp.concatenate([upper, sums[i2]], axis=1))
                        rights.append(jnp.concatenate([lower, turned[i2]], axis=1))
                lhs = jnp.concatenate([jnp.concatenate(l, axis=1) for l in lefts], axis=0)
                rhs = jnp.concatenate(rights, axis=0)
                made = jnp.dot(lhs, rhs, preferred_element_type=jnp.float32)
                total = made if total is None else total + made
            at = pl.ds(pl.multiple_of(base * 64, 64), 192)
            part[at, :] = part[at, :] + total
            return 0

        lax.fori_loop(lo, hi, body, 0)

    def arrived(offsets):
        for o in offsets:
            go_over(chip_at(o) * CORES + 1 - k).wait_recv()

    def invert():
        load_owner.wait()

        def body(s, _):
            inverse[s] = lax.fori_loop(0, n_col, lambda t, got: jnp.where(owner_ref[t] == s, t, got), 0, unroll=True)
            return 0

        lax.fori_loop(0, n_col, body, 0)

    part[...] = jnp.zeros_like(part)
    wide[...] = jnp.zeros_like(wide)
    masks()
    load_a.wait()
    turn()
    run = jnp.zeros((32, 128), jnp.float32)
    groups = slots // GROUP
    done = 0
    cooked = 0
    pending = [0]
    for d in range(1, half_ring):
        for c in range(CHUNKS):
            pass_on(d, c)
            if c == CHUNKS - 1:
                pending += [-d, d]
            spot_no = (d - 1) * CHUNKS + c
            if spot_no == 0:
                tables()
            elif spot_no == 1:
                invert()
            elif spot_no == 2:
                pass
            elif spot_no == 3:
                widen()
                for t in table_copies:
                    t.wait()
            elif done < groups:
                run = multiply(done, done + 1, run)
                done += 1
            elif len(pending) > 2 + 2 * (c == CHUNKS - 1):
                arrived(pending[:1])
                pending = pending[1:]
                dense(cooked, cooked + 1)
                cooked += 1
    if done < groups:
        run = multiply(done, groups, run)
    if pending[:-2]:
        arrived(pending[:-2])
        dense(cooked, cooked + len(pending) - 2)
        cooked += len(pending) - 2
    far_end()
    arrived(pending[-2:])
    dense(cooked, cooked + 2)

    lane_left = lax.broadcasted_iota(jnp.int32, (32, 128), 1) < 64
    first_core = k == 0
    early = row_width - 3

    def after_last(zz, xx):
        return chip_on(spot_of(zz, xx) + half_ring) * CORES * nb // per_agg + 3

    first_row = after_last(z, x)
    first_beside = after_last(beside // (width * CORES), lax.rem(beside // CORES, width))

    def halves(i, tile, lead):
        at = lax.rem(first_row + i, row_width) * 64
        lanes = slice(tile * 128, tile * 128 + 128)
        top = part[pl.ds(pl.multiple_of(at, 32), 32), lanes]
        low = part[pl.ds(pl.multiple_of(at + 32, 32), 32), lanes]
        if lead:
            return jnp.where(lane_left, top, jnp.concatenate([low[:, 64:128], low[:, 0:64]], axis=1))
        return jnp.where(lane_left, jnp.concatenate([top[:, 64:128], top[:, 0:64]], axis=1), low)

    ranges = [(0, early), (early, row_width)]

    def rows_of(ref, h):
        lo, hi = ranges[h]
        return ref.at[pl.ds(lo, hi - lo)]

    def scopy(h):
        return pltpu.make_async_remote_copy(
            src_ref=rows_of(edge_sib.at[0], h), dst_ref=rows_of(edge_sib.at[1], h),
            send_sem=ssend_sem.at[h], recv_sem=srecv_sem.at[h],
            device_id=(row, sibling), device_id_type=MESH,
        )

    def ecopy(r, w, h):
        return pltpu.make_async_remote_copy(
            src_ref=rows_of(edge_out, h), dst_ref=rows_of(edge_in.at[row], h),
            send_sem=esend_sem.at[w, h], recv_sem=erecv_sem.at[row, h],
            device_id=(r, beside), device_id_type=MESH,
        )

    def ecome(r, h):
        return pltpu.make_async_remote_copy(
            src_ref=rows_of(edge_out, h), dst_ref=rows_of(edge_in.at[r], h),
            send_sem=esend_sem.at[0, h], recv_sem=erecv_sem.at[r, h],
            device_id=(r, beside), device_id_type=MESH,
        )

    def mcopy(source, w, target, h):
        return pltpu.make_async_remote_copy(
            src_ref=rows_of(mid_in.at[source], h), dst_ref=rows_of(mid_in.at[source], h),
            send_sem=msend_sem.at[w, h], recv_sem=mrecv_sem.at[source, h],
            device_id=(target, me), device_id_type=MESH,
        )

    def send_edges(h):
        for i in range(*ranges[h]):
            e0 = halves(i, 0, True).astype(jnp.bfloat16)
            e2 = halves(i, 1, True).astype(jnp.bfloat16)
            edge_sib[0, i] = jnp.where(first_core, e2, e0)
            edge_out[i] = jnp.where(first_core, e0, e2)
        scopy(h).start()

        @pl.when(has_beside)
        def _():
            for w, r in enumerate(other_row + [row]):
                ecopy(r, w, h).start()

    def send_mid(h):
        mids = [halves(i, 0, False) for i in range(*ranges[h])]
        scopy(h).wait_recv()
        for i, value in zip(range(*ranges[h]), mids):
            mid_in[row, i] = (value + edge_sib[1, i].astype(jnp.float32)).astype(jnp.bfloat16)
        for w, o in enumerate(other_row):
            mcopy(row, w, o, h).start()

    @pl.when(jnp.logical_not(has_beside))
    def _():
        edge_in[...] = jnp.zeros_like(edge_in)

    send_edges(0)
    send_mid(0)
    arrived([half_ring])
    dense(cooked + 2, cooked + 3)
    send_edges(1)
    send_mid(1)
    for h in range(2):
        @pl.when(has_beside)
        def _():
            for r in [row] + other_row:
                ecome(r, h).wait_recv()

        for o in other_row:
            mcopy(o, 0, o, h).wait_recv()
    panel_agg = n_col // n_row
    for a in range(n_col):
        pieces = []
        for r in range(n_row):
            at = a - r * panel_agg + 1
            if 0 <= at < row_width:
                here = lax.rem(at - first_row + 2 * row_width, row_width)
                there = lax.rem(at - first_beside + 2 * row_width, row_width)
                pieces.append(mid_in[r, here].astype(jnp.float32) + edge_in[r, there].astype(jnp.float32))
        full[a] = functools.reduce(jnp.add, pieces).astype(jnp.bfloat16)

    def dcopy(s):
        return pltpu.make_async_remote_copy(
            src_ref=outgoing.at[s], dst_ref=incoming.at[me], send_sem=send_sem.at[s], recv_sem=recv2_sem.at[me],
            device_id=(row, s), device_id_type=MESH,
        )

    def post(i, _):
        s = jnp.where(z < DEPTH // 2, n_col - 1 - i, i)

        @pl.when(s != me)
        def _():
            outgoing[s] = full[inverse[s]]
            dcopy(s).start()

        return 0

    lax.fori_loop(0, n_col, post, 0)
    incoming[me] = full[inverse[me]]

    for d in range(half_ring):
        for c in range(CHUNKS):
            if d < half_ring - 1 or c < half:
                go_right(shard_at(-d), c).wait_send()
                go_left(shard_at(d), (c + half) % CHUNKS).wait_send()
    for i in range(chips):
        go_over(i * CORES + k).wait_send()
    for w, o in enumerate(other_row):
        pcopy(w, o).wait_send()
        for h in range(2):
            mcopy(row, w, o, h).wait_send()
    for h in range(2):
        scopy(h).wait_send()

    @pl.when(has_beside)
    def _():
        for w, r in enumerate(other_row + [row]):
            for h in range(2):
                ecopy(r, w, h).wait_send()

    def arrive(i, _):
        c = lax.rem(me + n_col - i, n_col)
        pltpu.make_async_remote_copy(
            src_ref=outgoing.at[0], dst_ref=incoming.at[c], send_sem=send_sem.at[c], recv_sem=recv2_sem.at[c],
            device_id=(row, c), device_id_type=MESH,
        ).wait_recv()
        return 0

    lax.fori_loop(1, n_col, arrive, 0)

    def sent(i, _):
        dcopy(lax.rem(me + i, n_col)).wait_send()
        return 0

    lax.fori_loop(1, n_col, sent, 0)


def unpack_kernel(blocks_ref, out_ref):
    for c in range(blocks_ref.shape[0]):
        block = blocks_ref[c].astype(jnp.float32)
        out_ref[0, c, 0:32, :] = block[:, 0:64]
        out_ref[0, c, 32:64, :] = block[:, 64:128]


def on_device(n_row, n_col, a_blocks, block_rows, block_cols, block_count, restrict, interp, aggregate, owner):
    vmem = pl.BlockSpec(memory_space=pltpu.VMEM)
    hbm = pl.BlockSpec(memory_space=pltpu.HBM)
    nb = restrict.shape[0]
    nj, piece = interp.shape[:2]
    slots = a_blocks.shape[2]
    agg_total = owner.shape[0]
    assert agg_total == n_col
    row_width = agg_total // n_row + 2
    bf16, f32, i32 = jnp.bfloat16, jnp.float32, jnp.int32
    chips = n_col // CORES
    panel = nb * n_col
    sized = jnp.transpose(a_blocks[0, 0], (1, 2, 0))
    dma = pltpu.SemaphoreType.DMA
    blocks = pl.pallas_call(
        functools.partial(coarse_kernel, n_row, n_col),
        out_shape=jax.ShapeDtypeStruct((n_col, 32, 128), bf16),
        in_specs=[hbm] * 8,
        out_specs=vmem,
        scratch_shapes=[
            pltpu.VMEM((1, slots), i32),
            pltpu.VMEM((1, slots), i32),
            pltpu.SMEM((1, 1), i32),
            pltpu.SMEM((aggregate.shape[0],), i32),
            pltpu.SMEM((agg_total,), i32),
            pltpu.VMEM((nb, 64, 64), bf16),
            pltpu.VMEM((nj, piece, 64), bf16),
            pltpu.VMEM((64, 64, slots), bf16),
            pltpu.VMEM((n_col, nb // 2, 64, 128), bf16),
            pltpu.VMEM((n_row, nj // 2, piece, 128), bf16),
            pltpu.VMEM((slots, 32, 128), bf16),
            pltpu.VMEM((nj, 128, 128), bf16),
            pltpu.VMEM((slots + 1, 32, 128), bf16),
            pltpu.VMEM((slots + 1, 32, 128), bf16),
            pltpu.VMEM((slots, 128), i32),
            pltpu.VMEM((slots, 128), i32),
            pltpu.VMEM((1, slots), i32),
            pltpu.VMEM((1, panel * 4), i32),
            pltpu.SMEM((1, slots), i32),
            pltpu.SMEM((1, panel * 4), i32),
            pltpu.VMEM((panel // 2, 3, 16, 128), bf16),
            pltpu.VMEM((row_width * 64, 256), f32),
            pltpu.VMEM((row_width, 32, 128), bf16),
            pltpu.VMEM((2, row_width, 32, 128), bf16),
            pltpu.VMEM((n_row, row_width, 32, 128), bf16),
            pltpu.VMEM((n_row, row_width, 32, 128), bf16),
            pltpu.VMEM((n_col, 32, 128), bf16),
            pltpu.VMEM((n_col, 32, 128), bf16),
            pltpu.SMEM((n_col,), i32),
            dma((8,)),
            dma((2,)),
            dma((n_col, CHUNKS)),
            dma((n_col, CHUNKS)),
            dma((n_col,)),
            dma((n_col, CHUNKS)),
            dma((n_row,)),
            dma((n_row,)),
            dma((2,)),
            dma((2,)),
            dma((n_row, 2)),
            dma((n_row, 2)),
            dma((n_row, 2)),
            dma((n_row, 2)),
            dma((n_col,)),
            dma((n_col,)),
        ],
        compiler_params=pltpu.CompilerParams(collective_id=0, has_side_effects=True, vmem_limit_bytes=55 * 2**20),
        name="coarse_operator",
    )(block_rows[0], block_cols[0], block_count, aggregate, owner, restrict, interp, sized)
    return pl.pallas_call(
        unpack_kernel,
        out_shape=jax.ShapeDtypeStruct((1, agg_total, 64, 64), f32),
        in_specs=[vmem],
        out_specs=vmem,
        name="unpack",
    )(blocks)


def solution(mesh):
    return jax.shard_map(
        functools.partial(on_device, mesh.shape["row"], mesh.shape["col"]),
        mesh=mesh,
        in_specs=(
            P("row", "col", None, None, None),
            P("row", "col", None),
            P("row", "col", None),
            P("row", "col"),
            P(("row", "col"), None, None),
            P("col", "row", None),
            P(),
            P(),
        ),
        out_specs=P("col", None, None, None),
        check_vma=False,
    )
```
